128 devices in a mesh: period: 4 (over x_hi, core), bus: 32 (over z, x_lo, y).
Axes of the slice: x: 4 (x_hi: 2, x_lo: 2; x = x_hi * 2 + x_lo), y: 4, z: 4, core: 2. Of those that a mesh axis runs over, the one named last changes fastest.
Arguments:
- gain: bfloat16 [4, 2048, 2048], P('period', 'bus'), may hold values from -0.15 to 1.15
- schur: bfloat16 [4, 2048, 2048], P('period', 'bus'), may hold values from -0.0625 to 0.0625
- inverse_blocks: bfloat16 [4, 10240, 320], P('period', 'bus'), may hold values from -0.3125 to 0.3125
- sensitivity: bfloat16 [10240, 2048], P('bus'), may hold values from -0.109375 to 0.109375
- residual_bus: float32 [4, 10240, 512], P('period', 'bus'), may hold values from -6 to 6
- unit_rhs: float32 [4, 2048, 512], P('period', 'bus'), may hold values from -6 to 6
- start_state: float32 [2048, 512], P('bus'), may hold values from -6 to 6
- active_set: int32 [4, 10240], P('period', 'bus'), may hold values 0 or 1
- unit_bus: int32 [2048], replicated, may hold values from 0 to 10239
Outputs:
- storage_path: float32 [4, 2048, 512], P('period', 'bus')
- costate: float32 [4, 2048, 512], P('period', 'bus')
- bus_update: float32 [4, 10240, 512], P('period', 'bus')
The draws below stay inside these ranges and needn't reach their ends.
All inputs are finite; a program needn't handle non-finite values. No bound on the sum of `active_set` on one device may be relied on, other than what follows from the above.
Results may differ from the reference program's by a relative error of at most 0.008.
Values may be sent and summed in bfloat16 or wider, within the bound.
A program may use at most 64 MiB of HBM per device.

```python
import math
import jax
import jax.numpy as jnp
from jax import lax

K = 2048
NB = 10240
R = 512
TIME_PERIODS = 4
BUS_DEV = 320
N_BUS = 32


def draw_gain(key, part):
    random_keys = jax.random.split(jax.random.fold_in(key, 17), 5)
    low_rate, high_rate = (0.02, 2.0)
    ramp_limit = jnp.exp(jax.random.uniform(random_keys[0], (1, K), jnp.float32, math.log(low_rate), math.log(high_rate)))
    regularizer_shift = 2.0 ** jax.random.uniform(random_keys[1], (TIME_PERIODS, 1), jnp.float32, -0.5, 0.5)
    surge_amount = jax.random.uniform(random_keys[2], (TIME_PERIODS, 1), jnp.float32) < 0.2
    cholesky_factor = jax.random.uniform(random_keys[3], (TIME_PERIODS, 1), jnp.float32, 0.5, 0.8)
    diagonal_entries = jnp.exp(-ramp_limit * regularizer_shift) * jnp.where(surge_amount, cholesky_factor, 1.0)
    spread = jnp.clip(jax.random.normal(random_keys[4], (TIME_PERIODS, K, K), jnp.float32), -4.0, 4.0) * (0.25 / math.sqrt(K))
    return (spread + jnp.eye(K, dtype=jnp.float32)[None] * diagonal_entries[:, :, None]).astype(jnp.bfloat16)


def place_ends(values, key, low, high):
    extent = values.shape
    index_at = [jax.random.randint(jax.random.fold_in(key, axis), (), 0, extent[axis]) for axis in range(len(extent))]
    values = values.at[tuple(index_at)].set(low)
    longest = extent.index(max(extent))
    index_at[longest] = (index_at[longest] + 1) % extent[longest]
    return values.at[tuple(index_at)].set(high)


def spiked(result, key, source, target, blocks, factor):
    def block_of(position):
        return (jnp.arange(result.shape[position]) // (result.shape[position] // blocks)).reshape((-1,) + (1,) * (result.ndim - 1 - position))

    near = jax.random.permutation(key, blocks)[block_of(target)]
    other_side = (block_of(target) + blocks // 2) % blocks
    return jnp.where((block_of(source) == near) | (block_of(source) == other_side), factor * result, result)


def levels(key, shape, pieces, least, largest):
    level, own = 1.0, jax.random.fold_in(key, 6)
    for dim, parts in pieces:
        heights = jnp.exp(jax.random.uniform(jax.random.fold_in(own, dim), (parts,), jnp.float32, least / len(pieces), largest / len(pieces)))
        level = level * jnp.repeat(heights, shape[dim] // parts).reshape([-1 if axis == dim else 1 for axis in range(len(shape))])
    return level


def noise(own_key, dims, scale, limit, shards=(), held_as=jnp.bfloat16):
    array = jax.random.normal(own_key, dims, jnp.float32) * scale
    if len(shards) > 0:
        array = levels(own_key, dims, shards, -0.22, 0.18) * array
    return jnp.clip(array, min=-limit, max=limit).astype(held_as)


def gaussian_with(key, dims, deviation, reach, shards, heavy, held_as=jnp.bfloat16):
    result = deviation * jax.random.normal(key, dims, jnp.float32)
    if shards:
        result = result * levels(key, dims, shards, -0.22, 0.18)
    return jnp.clip(spiked(result, jax.random.fold_in(key, 3), *heavy), -reach, reach).astype(held_as)


def setup_inputs(seed: int = 0) -> dict:
    streams_of = jax.random.split(jax.random.key(seed), 10)
    gain = draw_gain(jax.random.fold_in(streams_of[9], 71), 0)
    schur = noise(streams_of[1], (TIME_PERIODS, K, K), (4 * K) ** -0.5, 0.0625, ((0, 4), (1, 32)))
    inverse_blocks = noise(streams_of[2], (TIME_PERIODS, NB, BUS_DEV), (NB // N_BUS) ** -0.5, 0.3125, ((0, 4), (1, 32)))
    sensitivity = gaussian_with(streams_of[3], (NB, K), NB ** -0.5, 0.109375, ((0, 32),), (0, 1, 32, 2.75))
    residual_bus = noise(streams_of[4], (TIME_PERIODS, NB, R), 1.0, 6.0, ((0, 4), (1, 32)), jnp.float32)
    unit_rhs = noise(streams_of[5], (TIME_PERIODS, K, R), 1.0, 6.0, ((0, 4), (1, 32)), jnp.float32)
    start_state = noise(streams_of[6], (K, R), 1.0, 6.0, ((0, 32),), jnp.float32)
    active_set = place_ends((jax.random.randint(streams_of[7], (TIME_PERIODS, NB), 0, 4) < 1).astype(jnp.int32), jax.random.fold_in(streams_of[7], 1), 0, 1)
    unit_bus = place_ends(jax.random.randint(streams_of[8], (K,), 0, NB), jax.random.fold_in(streams_of[8], 1), 0, NB - 1).astype(jnp.int32)
    return {"gain": gain, "schur": schur, "inverse_blocks": inverse_blocks, "sensitivity": sensitivity, "residual_bus": residual_bus, "unit_rhs": unit_rhs, "start_state": start_state, "active_set": active_set, "unit_bus": unit_bus}


def partition_apply(blocks, values):
    rows = NB // N_BUS
    rounded = lax.optimization_barrier(values)
    grouped = rounded.astype(jnp.float32).reshape(N_BUS, rows, R)
    matrix = blocks.astype(jnp.float32).reshape(N_BUS, rows, rows)
    return jnp.einsum('qij,qjr->qir', matrix, grouped).reshape(NB, R)


def reference(gain, schur, inverse_blocks, sensitivity, residual_bus, unit_rhs, start_state, active_set, unit_bus):
    weighted = residual_bus * (1.0 + 3.0 * active_set[:, :, None].astype(jnp.float32))
    net_in = weighted.astype(jnp.bfloat16)
    unit_right = []
    for period in range(TIME_PERIODS):
        bus_solve = partition_apply(inverse_blocks[period], net_in[period]).astype(jnp.bfloat16)
        unit_right.append(unit_rhs[period] + jnp.dot(sensitivity.T, bus_solve, preferred_element_type=jnp.float32))
    later = jnp.zeros((K, R), jnp.float32)
    costates = [None] * TIME_PERIODS
    for period in reversed(range(TIME_PERIODS)):
        later = unit_right[period] + jnp.dot(gain[period].T, later.astype(jnp.bfloat16), preferred_element_type=jnp.float32)
        costates[period] = later
    current = start_state
    states = []
    updates = []
    for period in range(TIME_PERIODS):
        state_round = current.astype(jnp.bfloat16)
        costate_round = costates[period].astype(jnp.bfloat16)
        injection = jax.ops.segment_sum(state_round.astype(jnp.float32), unit_bus, num_segments=NB)
        network = (weighted[period] - injection).astype(jnp.bfloat16)
        updates.append(partition_apply(inverse_blocks[period], network))
        current = jnp.dot(gain[period], state_round, preferred_element_type=jnp.float32) - jnp.dot(schur[period], costate_round, preferred_element_type=jnp.float32)
        states.append(current)
    return jnp.stack(states), jnp.stack(costates), jnp.stack(updates)
```

```python
import jax
import jax.numpy as jnp
from jax import lax
from jax.experimental import pallas as pl
from jax.experimental.pallas import tpu as pltpu
from jax.sharding import PartitionSpec as P

MESH = pl.DeviceIdType.MESH
T = 4
X = 4
S = 16
F32 = jnp.float32
BF16 = jnp.bfloat16


def dot(a, b):
    return jnp.dot(a, b, preferred_element_type=F32)


def kernel(
    gain, schur, inverse, sens, resid, rhs, start, active, unit_bus,
    stor_out, cost_out, upd_out,
    sens_half, sens_t, resid_v, inv_v, act_v, ubus_v, start_v, start_b, weighted_v, solve_s, solve_r,
    gain_s, schur_s, gain_r, schur_r, gain_t, rhs_r, part_v, rs_s, rs_r, cost_v, cost_g, cost_p,
    state_v, state_g, full_v, full_r, onehot, inj_s, inj_r, upd_v,
    load_sem, sens_sem, solve_sem, gain_sem, schur_sem, rhs_sem, first_sem, rs_sem, cg_sem, xg_sem, pair_sem, full_sem,
    inj_sem, cout_sem, sout_sem, send_ring, send_plane,
):
    period = lax.axis_index("period")
    bus = lax.axis_index("bus")
    x_hi, core = lax.div(period, 2), lax.rem(period, 2)
    z, x_lo, y = lax.div(bus, 8), lax.rem(lax.div(bus, 4), 2), lax.rem(bus, 4)
    x = 2 * x_hi + x_lo
    spot = z * 4 + y
    x_pair = x + 1 - 2 * x_lo
    cols = 128

    def ring_id(xx, kk):
        return (2 * lax.div(xx, 2) + kk, z * 8 + lax.rem(xx, 2) * 4 + y)

    def plane_id(ss):
        return (period, lax.div(ss, 4) * 8 + x_lo * 4 + lax.rem(ss, 4))

    def lanes(xx):
        return pl.ds(pl.multiple_of(xx * cols, cols), cols)

    sent = []

    def ring_copy(src, dst, recv, xx, kk):
        send = send_ring.at[len(sent)]
        mine = (x == xx) & (core == kk)
        remote = pltpu.make_async_remote_copy(
            src_ref=src, dst_ref=dst, send_sem=send, recv_sem=recv, device_id=ring_id(xx, kk), device_id_type=MESH
        )

        @pl.when(mine)
        def _():
            pltpu.make_async_copy(src, dst, recv).start()

        @pl.when(jnp.logical_not(mine))
        def _():
            remote.start()

        sent.append((jnp.logical_not(mine), remote))

    def far_copy(src, dst, recv, xx, kk, on=None):
        send = send_ring.at[len(sent)]
        remote = pltpu.make_async_remote_copy(
            src_ref=src, dst_ref=dst, send_sem=send, recv_sem=recv, device_id=ring_id(xx, kk), device_id_type=MESH
        )
        if on is None:
            remote.start()
        else:
            pl.when(on)(remote.start)
        sent.append((on, remote))

    plane_sent = []

    def plane_copy(src_at, dst, recv):
        send = send_plane.at[len(plane_sent)]

        def one(i, carry):
            ss = lax.rem(spot + i, S)
            pltpu.make_async_remote_copy(
                src_ref=src_at(ss), dst_ref=dst, send_sem=send, recv_sem=recv, device_id=plane_id(ss), device_id_type=MESH
            ).start()
            return carry

        lax.fori_loop(1, S, one, 0)
        plane_sent.append(send)

    def plane_wait(buf, sem):
        some = buf.at[pl.ds(0, S - 1)]
        pltpu.make_async_copy(some, some, sem).wait()

    def landed(ref, sem):
        pltpu.make_async_copy(ref, ref, sem).wait()

    barrier = pltpu.get_barrier_semaphore()
    for i in range(1, 8):
        there = lax.rem(x * 2 + core + i, 8)
        pl.semaphore_signal(
            barrier, inc=1, device_id=ring_id(lax.div(there, 2), lax.rem(there, 2)), device_id_type=MESH
        )

    def greet(i, carry):
        pl.semaphore_signal(barrier, inc=1, device_id=plane_id(lax.rem(spot + i, S)), device_id_type=MESH)
        return carry

    lax.fori_loop(1, S, greet, 0)

    for i in range(4):
        strip = pl.ds(pl.multiple_of(i * 512 + core * 256, 256), 256)
        pltpu.make_async_copy(sens.at[:, strip], sens_half.at[x_lo, :, pl.ds(i * 256, 256)], load_sem.at[0]).start()
    load_resid = pltpu.make_async_copy(resid.at[0], resid_v, load_sem.at[1])
    load_inv = pltpu.make_async_copy(inverse.at[0], inv_v, load_sem.at[2])
    load_act = pltpu.make_async_copy(active, act_v, load_sem.at[3])
    load_start = pltpu.make_async_copy(start, start_v, load_sem.at[4])
    load_ubus = pltpu.make_async_copy(unit_bus, ubus_v, load_sem.at[5])
    for load in (load_resid, load_inv, load_act, load_start, load_ubus):
        load.start()
    for source, stage, sem in ((gain, gain_s, load_sem.at[6]), (schur, schur_s, load_sem.at[7])):
        for kk in range(2):
            for i in range(4):
                pltpu.make_async_copy(
                    source.at[0, :, pl.ds(i * 512 + kk * 256, 256)], stage.at[kk, :, pl.ds(i * 256, 256)], sem
                ).start()

    landed(sens_half.at[x_lo], load_sem.at[0])
    pl.semaphore_wait(barrier, 22)

    half = sens_half.shape[1] // 2
    for i, step in enumerate((1, X - 1)):
        rows = pl.ds(i * half, half)
        far_copy(
            sens_half.at[x_lo, rows], sens_half.at[x_lo, rows], sens_sem.at[i], lax.rem(x + step, X), core
        )

    load_resid.wait()
    load_inv.wait()
    load_act.wait()
    n = inv_v.shape[0]
    diagonal = lax.broadcasted_iota(jnp.int32, (n, n), 0) == lax.broadcasted_iota(jnp.int32, (n, n), 1)
    scale = 1.0 + 3.0 * act_v[...].astype(F32)
    scale = jnp.sum(jnp.where(diagonal, jnp.broadcast_to(scale, (n, n)), 0.0), axis=1, keepdims=True)
    weighted = resid_v[...] * scale
    weighted_v[...] = weighted
    solve_s[...] = dot(inv_v[...], weighted.astype(BF16)).astype(BF16)
    for xx in (0, 1, 2, 3):
        for kk in (0, 1):
            ring_copy(
                solve_s.at[:, lanes(xx)], solve_r.at[x_lo, :, lanes(period)], solve_sem.at[period * 2 + x_lo], xx, kk
            )

    load_start.wait()
    start_b[...] = start_v[...].astype(BF16)
    own = x_lo == core

    @pl.when(own)
    def _():
        state_g[0, spot] = start_b[:, lanes(x)]

    far_copy(start_b.at[:, lanes(x_pair)], state_g.at[0, spot], first_sem.at[0], x_pair, core, own)

    for xx in range(X):
        ring_copy(rhs.at[0, :, lanes(xx)], rhs_r.at[period], rhs_sem.at[period], xx, x_lo)

    landed(gain_s, load_sem.at[6])
    for xx in range(X):
        for kk in range(2):
            ring_copy(gain_s.at[kk], gain_r.at[period, x_lo], gain_sem.at[period * 2 + x_lo], xx, kk)

    @pl.when(jnp.logical_not(own))
    def _():
        landed(state_g.at[0, spot], first_sem.at[0])

    plane_copy(lambda ss: state_g.at[0, spot], state_g.at[0, spot], xg_sem.at[0])

    landed(schur_s, load_sem.at[7])
    for xx in range(X):
        for kk in range(2):
            ring_copy(schur_s.at[kk], schur_r.at[period, x_lo], schur_sem.at[period * 2 + x_lo], xx, kk)

    load_ubus.wait()
    for i in range(4):
        units = ubus_v[:, pl.ds(pl.multiple_of(i * 512 + core * 256, 256), 256)]
        for j in range(2):
            first = (z * 8 + j * 4 + y) * n
            ids = lax.broadcasted_iota(jnp.int32, (n, 256), 0) + first
            onehot[j * n : (j + 1) * n, i * 256 : (i + 1) * 256] = jnp.where(
                ids == jnp.broadcast_to(units, (n, 256)), 1.0, 0.0
            ).astype(BF16)

    for i in range(2):
        rows = pl.ds(i * half, half)
        landed(sens_half.at[1 - x_lo, rows], sens_sem.at[i])
    for j in range(2):
        sens_t[j] = sens_half[j].T
    for t in range(T):
        for j in range(2):
            landed(solve_r.at[j, :, lanes(t)], solve_sem.at[t * 2 + j])

    def reduce_start(t, partial):
        rs_s[t] = partial.astype(BF16).reshape(S, 64, cols)
        plane_copy(lambda ss: rs_s.at[t, ss], rs_r.at[t, spot], rs_sem.at[t])
        rs_r[t, spot] = rs_s[t, spot]

    last = (T - 1) * cols
    reduce_start(T - 1, dot(sens_t[0], solve_r[0, :, last:]) + dot(sens_t[1], solve_r[1, :, last:]))
    part_v[...] = dot(sens_t[0], solve_r[0, :, :last]) + dot(sens_t[1], solve_r[1, :, :last])

    for t in reversed(range(T)):
        if t < T - 1:
            for j in range(2):
                landed(gain_r.at[t, j], gain_sem.at[t * 2 + j])
                gain_t[t, :, j * 64 : (j + 1) * 64] = gain_r[t, j].T
            landed(cost_p.at[t + 1, 1 - core], pair_sem.at[t + 1])
            reduce_start(
                t, part_v[:, t * cols : (t + 1) * cols] + dot(gain_t[t], cost_p[t + 1].reshape(2 * 64, cols))
            )
            plane_copy(lambda ss, t=t: cost_g.at[t + 1, spot], cost_g.at[t + 1, spot], cg_sem.at[t + 1])
        landed(rhs_r.at[t], rhs_sem.at[t])
        plane_wait(rs_r.at[t], rs_sem.at[t])
        total = rhs_r[t] + jnp.sum(rs_r[t].astype(F32), axis=0)
        cost_v[t] = total
        rounded = total.astype(BF16)
        cost_g[t, spot] = rounded
        if t > 0:
            cost_p[t, core] = rounded
            far_copy(cost_g.at[t, spot], cost_p.at[t, core], pair_sem.at[t], x, 1 - core)
        else:
            plane_copy(lambda ss: cost_g.at[0, spot], cost_g.at[0, spot], cg_sem.at[0])
        ring_copy(cost_v.at[t], cost_out.at[0, :, lanes(x)], cout_sem.at[x], 2 * (t // 2) + core, t % 2)

    for t in range(T):
        for j in range(2):
            if t == T - 1:
                landed(gain_r.at[t, j], gain_sem.at[t * 2 + j])
            landed(schur_r.at[t, j], schur_sem.at[t * 2 + j])
        width = S * 64
        plane_wait(state_g.at[t], xg_sem.at[t])
        if t == T - 1:
            moved = dot(onehot[...], state_g[t].reshape(width, cols))
            inj_s[t] = moved.astype(BF16).reshape(2, n, cols)
            for j in range(2):
                ring_copy(
                    inj_s.at[t, j], inj_r.at[core, :, lanes(x)], inj_sem.at[x * 2 + core], 2 * (t // 2) + j, t % 2
                )
        plane_wait(cost_g.at[t], cg_sem.at[t])
        full = dot(gain_r[t].reshape(2 * 64, width), state_g[t].reshape(width, cols)) - dot(
            schur_r[t].reshape(2 * 64, width), cost_g[t].reshape(width, cols)
        )
        full_v[t] = full.reshape(2, 64, cols)
        far_copy(full_v.at[t, 1 - core], full_r.at[t], full_sem.at[t], x, 1 - core)
        if t < T - 1:
            moved = dot(onehot[...], state_g[t].reshape(width, cols))
            inj_s[t] = moved.astype(BF16).reshape(2, n, cols)
        landed(full_r.at[t], full_sem.at[t])
        total = full_v[t, core] + full_r[t]
        state_v[t] = total
        if t < T - 1:
            state_g[t + 1, spot] = total.astype(BF16)
            plane_copy(lambda ss, t=t: state_g.at[t + 1, spot], state_g.at[t + 1, spot], xg_sem.at[t + 1])
        ring_copy(state_v.at[t], stor_out.at[0, :, lanes(x)], sout_sem.at[x], 2 * (t // 2) + core, t % 2)
        if t < T - 1:
            for j in range(2):
                ring_copy(
                    inj_s.at[t, j], inj_r.at[core, :, lanes(x)], inj_sem.at[x * 2 + core], 2 * (t // 2) + j, t % 2
                )

    for xx in range(X):
        for kk in range(2):
            landed(inj_r.at[kk, :, lanes(xx)], inj_sem.at[xx * 2 + kk])
    network = weighted_v[...] - (inj_r[0].astype(F32) + inj_r[1].astype(F32))
    upd_v[...] = dot(inv_v[...], network.astype(BF16))
    store = pltpu.make_async_copy(upd_v, upd_out.at[0], load_sem.at[8])
    store.start()
    for xx in range(X):
        landed(cost_out.at[0, :, lanes(xx)], cout_sem.at[xx])
        landed(stor_out.at[0, :, lanes(xx)], sout_sem.at[xx])
    for on, copy in sent:
        if on is None:
            copy.wait_send()
        else:
            pl.when(on)(copy.wait_send)
    for send in plane_sent:
        plane_wait(rs_s.at[0], send)
    store.wait()


def body(gain, schur, inverse_blocks, sensitivity, residual_bus, unit_rhs, start_state, active_set, unit_bus):
    anywhere = pl.BlockSpec(memory_space=pl.ANY)
    n = inverse_blocks.shape[1]
    dma = pltpu.SemaphoreType.DMA
    scratch = [
        pltpu.VMEM((2, n, 1024), BF16),
        pltpu.VMEM((2, 1024, n), BF16),
        pltpu.VMEM((n, 512), F32),
        pltpu.VMEM((n, n), BF16),
        pltpu.VMEM((1, n), jnp.int32),
        pltpu.VMEM((1, 2048), jnp.int32),
        pltpu.VMEM((64, 512), F32),
        pltpu.VMEM((64, 512), BF16),
        pltpu.VMEM((n, 512), F32),
        pltpu.VMEM((n, 512), BF16),
        pltpu.VMEM((2, n, 512), BF16),
        pltpu.VMEM((2, 64, 1024), BF16),
        pltpu.VMEM((2, 64, 1024), BF16),
        pltpu.VMEM((T, 2, 64, 1024), BF16),
        pltpu.VMEM((T, 2, 64, 1024), BF16),
        pltpu.VMEM((T - 1, 1024, 128), BF16),
        pltpu.VMEM((T, 64, 128), F32),
        pltpu.VMEM((1024, 384), F32),
        pltpu.VMEM((T, S, 64, 128), BF16),
        pltpu.VMEM((T, S, 64, 128), BF16),
        pltpu.VMEM((T, 64, 128), F32),
        pltpu.VMEM((T, S, 64, 128), BF16),
        pltpu.VMEM((T, 2, 64, 128), BF16),
        pltpu.VMEM((T, 64, 128), F32),
        pltpu.VMEM((T, S, 64, 128), BF16),
        pltpu.VMEM((T, 2, 64, 128), F32),
        pltpu.VMEM((T, 64, 128), F32),
        pltpu.VMEM((2 * n, 1024), BF16),
        pltpu.VMEM((T, 2, n, 128), BF16),
        pltpu.VMEM((2, n, 512), BF16),
        pltpu.VMEM((n, 512), F32),
        dma((9,)),
        dma((2,)),
        dma((8,)),
        dma((8,)),
        dma((8,)),
        dma((4,)),
        dma((1,)),
        dma((4,)),
        dma((4,)),
        dma((4,)),
        dma((4,)),
        dma((4,)),
        dma((8,)),
        dma((4,)),
        dma((4,)),
        dma((64,)),
        dma((12,)),
    ]
    return pl.pallas_call(
        kernel,
        out_shape=(
            jax.ShapeDtypeStruct((1, 64, 512), F32),
            jax.ShapeDtypeStruct((1, 64, 512), F32),
            jax.ShapeDtypeStruct((1, n, 512), F32),
        ),
        in_specs=[anywhere] * 9,
        out_specs=(anywhere,) * 3,
        scratch_shapes=scratch,
        compiler_params=pltpu.CompilerParams(
            collective_id=0, has_side_effects=True, vmem_limit_bytes=48 * 1024 * 1024
        ),
    )(
        gain, schur, inverse_blocks, sensitivity, residual_bus, unit_rhs, start_state, active_set,
        unit_bus.reshape(1, -1),
    )


def solution(mesh):
    placed = (
        P("period", "bus", None),
        P("period", "bus", None),
        P("period", "bus", None),
        P("bus", None),
        P("period", "bus", None),
        P("period", "bus", None),
        P("bus", None),
        P("period", "bus"),
        P(),
    )
    return jax.shard_map(
        body,
        mesh=mesh,
        in_specs=placed,
        out_specs=(P("period", "bus", None), P("period", "bus", None), P("period", "bus", None)),
        check_vma=False,
    )
```

```python
import jax
import jax.numpy as jnp
from jax import lax
from jax.experimental import pallas as pl
from jax.experimental.pallas import tpu as pltpu
from jax.sharding import PartitionSpec as P

MESH = pl.DeviceIdType.MESH
T = 4
X = 4
S = 16
F32 = jnp.float32
BF16 = jnp.bfloat16


def dot(a, b):
    return jnp.dot(a, b, preferred_element_type=F32)


def kernel(
    gain, schur, inverse, sens, resid, rhs, start, active, unit_bus,
    stor_out, cost_out, upd_out,
    sens_half, sens_t, resid_v, inv_v, act_v, ubus_v, start_v, start_b, weighted_v, solve_s, solve_r,
    gain_s, schur_s, gain_r, schur_r, gain_t, rhs_r, part_v, rs_s, rs_r, cost_v, cost_g, cost_p,
    state_v, state_g, full_v, full_r, onehot, inj_s, inj_r, upd_v,
    load_sem, sens_sem, solve_sem, gain_sem, schur_sem, rhs_sem, first_sem, rs_sem, cg_sem, xg_sem, pair_sem, full_sem,
    inj_sem, cout_sem, sout_sem, send_ring, send_plane,
):
    period = lax.axis_index("period")
    bus = lax.axis_index("bus")
    x_hi, core = lax.div(period, 2), lax.rem(period, 2)
    z, x_lo, y = lax.div(bus, 8), lax.rem(lax.div(bus, 4), 2), lax.rem(bus, 4)
    x = 2 * x_hi + x_lo
    spot = z * 4 + y
    x_pair = x + 1 - 2 * x_lo
    cols = 128

    def ring_id(xx, kk):
        return (2 * lax.div(xx, 2) + kk, z * 8 + lax.rem(xx, 2) * 4 + y)

    def plane_id(ss):
        return (period, lax.div(ss, 4) * 8 + x_lo * 4 + lax.rem(ss, 4))

    def lanes(xx):
        return pl.ds(pl.multiple_of(xx * cols, cols), cols)

    pend = {}
    started = set()
    sent = []

    def ring_copy(src, dst, recv, xx, kk):
        send = send_ring.at[len(sent)]
        mine = (x == xx) & (core == kk)
        remote = pltpu.make_async_remote_copy(
            src_ref=src, dst_ref=dst, send_sem=send, recv_sem=recv, device_id=ring_id(xx, kk), device_id_type=MESH
        )

        @pl.when(mine)
        def _():
            pltpu.make_async_copy(src, dst, recv).start()

        @pl.when(jnp.logical_not(mine))
        def _():
            remote.start()

        sent.append((jnp.logical_not(mine), remote))

    def ring_group(name, copies):
        made = []
        for src, dst, recv, xx, kk in copies:
            mine = (x == xx) & (core == kk)
            remote = pltpu.make_async_remote_copy(
                src_ref=src, dst_ref=dst, send_sem=send_ring.at[len(sent)], recv_sem=recv,
                device_id=ring_id(xx, kk), device_id_type=MESH,
            )
            made.append((mine, remote, pltpu.make_async_copy(src, dst, recv)))
            sent.append([jnp.logical_not(mine), remote, []])
        mark = sent[-len(made):]

        def start(*periods):
            for m in mark:
                m[2].extend(periods)
            for p in periods:
                started.add((name, p))
            on = period == periods[0]
            for p in periods[1:]:
                on = on | (period == p)
            @pl.when(on)
            def _():
                for mine, remote, local in made:
                    pl.when(mine)(local.start)
                    pl.when(jnp.logical_not(mine))(remote.start)

        return start

    def far_copy(src, dst, recv, xx, kk, on=None):
        send = send_ring.at[len(sent)]
        remote = pltpu.make_async_remote_copy(
            src_ref=src, dst_ref=dst, send_sem=send, recv_sem=recv, device_id=ring_id(xx, kk), device_id_type=MESH
        )
        if on is None:
            remote.start()
        else:
            pl.when(on)(remote.start)
        sent.append((on, remote))

    plane_sent = []

    def plane_copy(src_at, dst, recv):
        send = send_plane.at[len(plane_sent)]

        def one(i, carry):
            ss = lax.rem(spot + i, S)
            pltpu.make_async_remote_copy(
                src_ref=src_at(ss), dst_ref=dst, send_sem=send, recv_sem=recv, device_id=plane_id(ss), device_id_type=MESH
            ).start()
            return carry

        lax.fori_loop(1, S, one, 0)
        plane_sent.append(send)

    def plane_wait(buf, sem):
        some = buf.at[pl.ds(0, S - 1)]
        pltpu.make_async_copy(some, some, sem).wait()

    def landed(ref, sem):
        pltpu.make_async_copy(ref, ref, sem).wait()

    def take(key):
        pend.pop(key)()

    def home_wait(t, fn0):
        def fn():
            fn0()

        pl.when(period == t)(fn)

    def inj_wait():
        for xx in range(X):
            for kk in range(2):
                landed(inj_r.at[kk, :, lanes(xx)], inj_sem.at[xx * 2 + kk])

    barrier = pltpu.get_barrier_semaphore()
    for i in range(1, 8):
        there = lax.rem(x * 2 + core + i, 8)
        pl.semaphore_signal(
            barrier, inc=1, device_id=ring_id(lax.div(there, 2), lax.rem(there, 2)), device_id_type=MESH
        )

    def greet(i, carry):
        pl.semaphore_signal(barrier, inc=1, device_id=plane_id(lax.rem(spot + i, S)), device_id_type=MESH)
        return carry

    lax.fori_loop(1, S, greet, 0)

    for i in range(4):
        strip = pl.ds(pl.multiple_of(i * 512 + core * 256, 256), 256)
        pltpu.make_async_copy(sens.at[:, strip], sens_half.at[x_lo, :, pl.ds(i * 256, 256)], load_sem.at[0]).start()
    load_resid = pltpu.make_async_copy(resid.at[0], resid_v, load_sem.at[1])
    load_inv = pltpu.make_async_copy(inverse.at[0], inv_v, load_sem.at[2])
    load_act = pltpu.make_async_copy(active, act_v, load_sem.at[3])
    load_start = pltpu.make_async_copy(start, start_v, load_sem.at[4])
    load_ubus = pltpu.make_async_copy(unit_bus, ubus_v, load_sem.at[5])
    for load in (load_resid, load_inv, load_act, load_start, load_ubus):
        load.start()
    for source, stage, sem in ((gain, gain_s, load_sem.at[6]), (schur, schur_s, load_sem.at[7])):
        for kk in range(2):
            for i in range(4):
                pltpu.make_async_copy(
                    source.at[0, :, pl.ds(i * 512 + kk * 256, 256)], stage.at[kk, :, pl.ds(i * 256, 256)], sem
                ).start()

    pend['load_resid'] = load_resid.wait
    pend['load_inv'] = load_inv.wait
    pend['load_act'] = load_act.wait
    pend['load_start'] = load_start.wait
    pend['load_ubus'] = load_ubus.wait
    pend['gain_s'] = lambda: landed(gain_s, load_sem.at[6])
    pend['schur_s'] = lambda: landed(schur_s, load_sem.at[7])
    take('load_resid')
    take('load_inv')
    take('load_act')
    n = inv_v.shape[0]
    diagonal = lax.broadcasted_iota(jnp.int32, (n, n), 0) == lax.broadcasted_iota(jnp.int32, (n, n), 1)
    scale = 1.0 + 3.0 * act_v[...].astype(F32)
    scale = jnp.sum(jnp.where(diagonal, jnp.broadcast_to(scale, (n, n)), 0.0), axis=1, keepdims=True)
    weighted = resid_v[...] * scale
    weighted_v[...] = weighted
    solve_s[...] = dot(inv_v[...], weighted.astype(BF16)).astype(BF16)
    landed(sens_half.at[x_lo], load_sem.at[0])
    pl.semaphore_wait(barrier, 22)

    half = sens_half.shape[1] // 2
    for i, step in enumerate((1, X - 1)):
        rows = pl.ds(i * half, half)
        far_copy(
            sens_half.at[x_lo, rows], sens_half.at[x_lo, rows], sens_sem.at[i], lax.rem(x + step, X), core
        )

    def sens_wait():
        for i in range(2):
            rows = pl.ds(i * half, half)
            landed(sens_half.at[1 - x_lo, rows], sens_sem.at[i])

    pend['sens'] = sens_wait

    line = [(xx, kk) for xx in range(X) for kk in range(2)]
    send_solve = ring_group('solve', [
        (solve_s.at[:, lanes(xx)], solve_r.at[x_lo, :, lanes(period)], solve_sem.at[period * 2 + x_lo], xx, kk)
        for xx, kk in line
    ])
    send_gain = ring_group('gain', [
        (gain_s.at[kk], gain_r.at[period, x_lo], gain_sem.at[period * 2 + x_lo], xx, kk) for xx, kk in line
    ])
    send_schur = ring_group('schur', [
        (schur_s.at[kk], schur_r.at[period, x_lo], schur_sem.at[period * 2 + x_lo], xx, kk) for xx, kk in line
    ])
    send_solve(3)

    for t in range(T):
        for j in range(2):
            pend[f'solve{t}{j}'] = lambda t=t, j=j: landed(solve_r.at[j, :, lanes(t)], solve_sem.at[t * 2 + j])
    take('load_start')
    start_b[...] = start_v[...].astype(BF16)
    own = x_lo == core

    @pl.when(own)
    def _():
        state_g[0, spot] = start_b[:, lanes(x)]

    far_copy(start_b.at[:, lanes(x_pair)], state_g.at[0, spot], first_sem.at[0], x_pair, core, own)

    def first_wait():
        @pl.when(jnp.logical_not(own))
        def _():
            landed(state_g.at[0, spot], first_sem.at[0])

    pend['first'] = first_wait
    for t in range(T):
        pend[f'rhs{t}'] = lambda t=t: landed(rhs_r.at[t], rhs_sem.at[t])
    for xx in range(X):
        ring_copy(rhs.at[0, :, lanes(xx)], rhs_r.at[period], rhs_sem.at[period], xx, x_lo)

    for t in range(T):
        for j in range(2):
            pend[f'gain{t}{j}'] = lambda t=t, j=j: landed(gain_r.at[t, j], gain_sem.at[t * 2 + j])
    take('first')
    pend['xg0'] = lambda: plane_wait(state_g.at[0], xg_sem.at[0])
    plane_copy(lambda ss: state_g.at[0, spot], state_g.at[0, spot], xg_sem.at[0])

    for t in range(T):
        for j in range(2):
            pend[f'schur{t}{j}'] = lambda t=t, j=j: landed(schur_r.at[t, j], schur_sem.at[t * 2 + j])
    take('load_ubus')
    for i in range(4):
        units = ubus_v[:, pl.ds(pl.multiple_of(i * 512 + core * 256, 256), 256)]
        for j in range(2):
            first = (z * 8 + j * 4 + y) * n
            ids = lax.broadcasted_iota(jnp.int32, (n, 256), 0) + first
            onehot[j * n : (j + 1) * n, i * 256 : (i + 1) * 256] = jnp.where(
                ids == jnp.broadcast_to(units, (n, 256)), 1.0, 0.0
            ).astype(BF16)

    take('sens')
    take('gain_s')
    take('schur_s')
    send_solve(0, 1, 2)
    send_gain(2)
    for j in range(2):
        sens_t[j] = sens_half[j].T
    take('solve30')
    take('solve31')

    def reduce_start(t, partial):
        pend[f'rs{t}'] = lambda: plane_wait(rs_r.at[t], rs_sem.at[t])
        rs_s[t] = partial.astype(BF16).reshape(S, 64, cols)
        plane_copy(lambda ss: rs_s.at[t, ss], rs_r.at[t, spot], rs_sem.at[t])
        rs_r[t, spot] = rs_s[t, spot]

    last = (T - 1) * cols
    reduce_start(T - 1, dot(sens_t[0], solve_r[0, :, last:]) + dot(sens_t[1], solve_r[1, :, last:]))
    send_gain(1)
    for t in range(T - 1):
        for j in range(2):
            take(f'solve{t}{j}')
    part_v[...] = dot(sens_t[0], solve_r[0, :, :last]) + dot(sens_t[1], solve_r[1, :, :last])

    def send_cg(t):
        pend[f'cg{t}'] = lambda: plane_wait(cost_g.at[t], cg_sem.at[t])
        plane_copy(lambda ss: cost_g.at[t, spot], cost_g.at[t, spot], cg_sem.at[t])

    for t in reversed(range(T)):
        if t < T - 1:
            for j in range(2):
                take(f'gain{t}{j}')
                gain_t[t, :, j * 64 : (j + 1) * 64] = gain_r[t, j].T
            take(f'pair{t + 1}')
            reduce_start(
                t, part_v[:, t * cols : (t + 1) * cols] + dot(gain_t[t], cost_p[t + 1].reshape(2 * 64, cols))
            )
        take(f'rhs{t}')
        take(f'rs{t}')
        total = rhs_r[t] + jnp.sum(rs_r[t].astype(F32), axis=0)
        cost_v[t] = total
        rounded = total.astype(BF16)
        cost_g[t, spot] = rounded
        if t > 0:
            cost_p[t, core] = rounded
            pend[f'pair{t}'] = lambda t=t: landed(cost_p.at[t, 1 - core], pair_sem.at[t])
            far_copy(cost_g.at[t, spot], cost_p.at[t, core], pair_sem.at[t], x, 1 - core)
        else:
            send_cg(0)
            send_cg(1)
        pend[f'cout{t}'] = lambda t=t: home_wait(t, lambda: [landed(cost_out.at[0, :, lanes(xx)], cout_sem.at[xx]) for xx in range(X)])
        ring_copy(cost_v.at[t], cost_out.at[0, :, lanes(x)], cout_sem.at[x], 2 * (t // 2) + core, t % 2)
        if t == 3:
            send_gain(0)
        elif t == 2:
            send_schur(0)
        elif t == 1:
            send_schur(1)
        else:
            send_schur(2)

    for t in range(T):
        for j in range(2):
            if t == T - 1:
                take(f'gain{t}{j}')
            take(f'schur{t}{j}')
        width = S * 64
        take(f'xg{t}')
        if t == T - 1:
            moved = dot(onehot[...], state_g[t].reshape(width, cols))
            inj_s[t] = moved.astype(BF16).reshape(2, n, cols)
            for j in range(2):
                pend[f'inj{t}'] = lambda t=t: home_wait(t, inj_wait)
                ring_copy(
                    inj_s.at[t, j], inj_r.at[core, :, lanes(x)], inj_sem.at[x * 2 + core], 2 * (t // 2) + j, t % 2
                )
        take(f'cg{t}')
        full = dot(gain_r[t].reshape(2 * 64, width), state_g[t].reshape(width, cols)) - dot(
            schur_r[t].reshape(2 * 64, width), cost_g[t].reshape(width, cols)
        )
        full_v[t] = full.reshape(2, 64, cols)
        pend[f'full{t}'] = lambda t=t: landed(full_r.at[t], full_sem.at[t])
        far_copy(full_v.at[t, 1 - core], full_r.at[t], full_sem.at[t], x, 1 - core)
        take(f'full{t}')
        total = full_v[t, core] + full_r[t]
        state_v[t] = total
        if t < T - 1:
            state_g[t + 1, spot] = total.astype(BF16)
            pend[f'xg{t + 1}'] = lambda t=t: plane_wait(state_g.at[t + 1], xg_sem.at[t + 1])
            plane_copy(lambda ss, t=t: state_g.at[t + 1, spot], state_g.at[t + 1, spot], xg_sem.at[t + 1])
            if t + 2 < T:
                send_cg(t + 2)
        pend[f'sout{t}'] = lambda t=t: home_wait(t, lambda: [landed(stor_out.at[0, :, lanes(xx)], sout_sem.at[xx]) for xx in range(X)])
        ring_copy(state_v.at[t], stor_out.at[0, :, lanes(x)], sout_sem.at[x], 2 * (t // 2) + core, t % 2)
        if t == 0:
            send_gain(3)
            send_schur(3)
        if t < T - 1:
            moved = dot(onehot[...], state_g[t].reshape(width, cols))
            inj_s[t] = moved.astype(BF16).reshape(2, n, cols)
            for j in range(2):
                pend[f'inj{t}'] = lambda t=t: home_wait(t, inj_wait)
                ring_copy(
                    inj_s.at[t, j], inj_r.at[core, :, lanes(x)], inj_sem.at[x * 2 + core], 2 * (t // 2) + j, t % 2
                )

    for t in range(T):
        take(f'inj{t}')
    network = weighted_v[...] - (inj_r[0].astype(F32) + inj_r[1].astype(F32))
    upd_v[...] = dot(inv_v[...], network.astype(BF16))
    store = pltpu.make_async_copy(upd_v, upd_out.at[0], load_sem.at[8])
    store.start()
    for t in range(T):
        take(f'cout{t}')
        take(f'sout{t}')
    store.wait()

    for key in list(pend):
        take(key)
    for on, copy, *more in sent:
        if more:
            if not more[0]:
                continue
            had = period == more[0][0]
            for p in more[0][1:]:
                had = had | (period == p)
            on = on & had
        if on is None:
            copy.wait_send()
        else:
            pl.when(on)(copy.wait_send)
    for send in plane_sent:
        plane_wait(rs_s.at[0], send)


def body(gain, schur, inverse_blocks, sensitivity, residual_bus, unit_rhs, start_state, active_set, unit_bus):
    anywhere = pl.BlockSpec(memory_space=pl.ANY)
    n = inverse_blocks.shape[1]
    dma = pltpu.SemaphoreType.DMA
    scratch = [
        pltpu.VMEM((2, n, 1024), BF16),
        pltpu.VMEM((2, 1024, n), BF16),
        pltpu.VMEM((n, 512), F32),
        pltpu.VMEM((n, n), BF16),
        pltpu.VMEM((1, n), jnp.int32),
        pltpu.VMEM((1, 2048), jnp.int32),
        pltpu.VMEM((64, 512), F32),
        pltpu.VMEM((64, 512), BF16),
        pltpu.VMEM((n, 512), F32),
        pltpu.VMEM((n, 512), BF16),
        pltpu.VMEM((2, n, 512), BF16),
        pltpu.VMEM((2, 64, 1024), BF16),
        pltpu.VMEM((2, 64, 1024), BF16),
        pltpu.VMEM((T, 2, 64, 1024), BF16),
        pltpu.VMEM((T, 2, 64, 1024), BF16),
        pltpu.VMEM((T - 1, 1024, 128), BF16),
        pltpu.VMEM((T, 64, 128), F32),
        pltpu.VMEM((1024, 384), F32),
        pltpu.VMEM((T, S, 64, 128), BF16),
        pltpu.VMEM((T, S, 64, 128), BF16),
        pltpu.VMEM((T, 64, 128), F32),
        pltpu.VMEM((T, S, 64, 128), BF16),
        pltpu.VMEM((T, 2, 64, 128), BF16),
        pltpu.VMEM((T, 64, 128), F32),
        pltpu.VMEM((T, S, 64, 128), BF16),
        pltpu.VMEM((T, 2, 64, 128), F32),
        pltpu.VMEM((T, 64, 128), F32),
        pltpu.VMEM((2 * n, 1024), BF16),
        pltpu.VMEM((T, 2, n, 128), BF16),
        pltpu.VMEM((2, n, 512), BF16),
        pltpu.VMEM((n, 512), F32),
        dma((9,)),
        dma((2,)),
        dma((8,)),
        dma((8,)),
        dma((8,)),
        dma((4,)),
        dma((1,)),
        dma((4,)),
        dma((4,)),
        dma((4,)),
        dma((4,)),
        dma((4,)),
        dma((8,)),
        dma((4,)),
        dma((4,)),
        dma((64,)),
        dma((12,)),
    ]
    return pl.pallas_call(
        kernel,
        out_shape=(
            jax.ShapeDtypeStruct((1, 64, 512), F32),
            jax.ShapeDtypeStruct((1, 64, 512), F32),
            jax.ShapeDtypeStruct((1, n, 512), F32),
        ),
        in_specs=[anywhere] * 9,
        out_specs=(anywhere,) * 3,
        scratch_shapes=scratch,
        compiler_params=pltpu.CompilerParams(
            collective_id=0, has_side_effects=True, vmem_limit_bytes=60 * 1024 * 1024
        ),
    )(
        gain, schur, inverse_blocks, sensitivity, residual_bus, unit_rhs, start_state, active_set,
        unit_bus.reshape(1, -1),
    )


def solution(mesh):
    placed = (
        P("period", "bus", None),
        P("period", "bus", None),
        P("period", "bus", None),
        P("bus", None),
        P("period", "bus", None),
        P("period", "bus", None),
        P("bus", None),
        P("period", "bus"),
        P(),
    )
    return jax.shard_map(
        body,
        mesh=mesh,
        in_specs=placed,
        out_specs=(P("period", "bus", None), P("period", "bus", None), P("period", "bus", None)),
        check_vma=False,
    )
```

```python
import jax
import jax.numpy as jnp
from jax import lax
from jax.experimental import pallas as pl
from jax.experimental.pallas import tpu as pltpu
from jax.sharding import PartitionSpec as P

MESH = pl.DeviceIdType.MESH
T = 4
X = 4
S = 16
F32 = jnp.float32
OTHERS = sorted(
    ((dz, dy) for dz in range(4) for dy in range(4) if dz or dy), key=lambda d: -min(d[0], 4 - d[0]) - min(d[1], 4 - d[1])
)
BF16 = jnp.bfloat16


def dot(a, b):
    return jnp.dot(a, b, preferred_element_type=F32)


def kernel(
    gain, schur, inverse, sens, resid, rhs, start, active, unit_bus,
    stor_out, cost_out, network_out,
    sens_half, sens_t, resid_v, inv_v, act_v, ubus_v, start_v, start_b, weighted_v, solve_s, solve_r,
    gain_s, schur_s, gain_r, schur_r, gain_t, rhs_r, part_v, rs_s, rs_r, cost_v, cost_g, cost_p,
    state_v, state_g, full_v, full_r, onehot, inj_s, inj_r, network_v,
    load_sem, sens_sem, solve_sem, swap_sem, gain_sem, schur_sem, rhs_sem, first_sem, rs_sem, cg_sem, xg_sem, pair_sem, full_sem,
    inj_sem, cout_sem, sout_sem, send_ring, send_plane,
):
    period = lax.axis_index("period")
    bus = lax.axis_index("bus")
    x_hi, core = lax.div(period, 2), lax.rem(period, 2)
    z, x_lo, y = lax.div(bus, 8), lax.rem(lax.div(bus, 4), 2), lax.rem(bus, 4)
    x = 2 * x_hi + x_lo
    spot = z * 4 + y
    x_pair = x + 1 - 2 * x_lo
    cols = 128

    def ring_id(xx, kk):
        return (2 * lax.div(xx, 2) + kk, z * 8 + lax.rem(xx, 2) * 4 + y)

    def plane_id(ss):
        return (period, lax.div(ss, 4) * 8 + x_lo * 4 + lax.rem(ss, 4))

    def plane_spot(dz, dy):
        return lax.rem(z + dz, 4) * 4 + lax.rem(y + dy, 4)

    def lanes(xx):
        return pl.ds(pl.multiple_of(xx * cols, cols), cols)

    pend = {}
    started = set()
    sent = []

    def ring_copy(src, dst, recv, xx, kk):
        send = send_ring.at[len(sent)]
        mine = (x == xx) & (core == kk)
        remote = pltpu.make_async_remote_copy(
            src_ref=src, dst_ref=dst, send_sem=send, recv_sem=recv, device_id=ring_id(xx, kk), device_id_type=MESH
        )

        @pl.when(mine)
        def _():
            pltpu.make_async_copy(src, dst, recv).start()

        @pl.when(jnp.logical_not(mine))
        def _():
            remote.start()

        sent.append((jnp.logical_not(mine), remote))

    def ring_group(name, copies):
        made = []
        for src, dst, recv, xx, kk in copies:
            mine = (x == xx) & (core == kk)
            remote = pltpu.make_async_remote_copy(
                src_ref=src, dst_ref=dst, send_sem=send_ring.at[len(sent)], recv_sem=recv,
                device_id=ring_id(xx, kk), device_id_type=MESH,
            )
            made.append((mine, remote, pltpu.make_async_copy(src, dst, recv)))
            sent.append([jnp.logical_not(mine), remote, []])
        mark = sent[-len(made):]

        def start(*periods):
            for m in mark:
                m[2].extend(periods)
            for p in periods:
                started.add((name, p))
            on = period == periods[0]
            for p in periods[1:]:
                on = on | (period == p)
            @pl.when(on)
            def _():
                for mine, remote, local in made:
                    pl.when(mine)(local.start)
                    pl.when(jnp.logical_not(mine))(remote.start)

        return start

    def far_copy(src, dst, recv, xx, kk, on=None):
        send = send_ring.at[len(sent)]
        remote = pltpu.make_async_remote_copy(
            src_ref=src, dst_ref=dst, send_sem=send, recv_sem=recv, device_id=ring_id(xx, kk), device_id_type=MESH
        )
        if on is None:
            remote.start()
        else:
            pl.when(on)(remote.start)
        sent.append((on, remote))

    plane_sent = []

    def plane_copy(src_at, dst, recv):
        send = send_plane.at[len(plane_sent)]

        for dz, dy in OTHERS:
            ss = plane_spot(dz, dy)
            pltpu.make_async_remote_copy(
                src_ref=src_at(ss), dst_ref=dst, send_sem=send, recv_sem=recv, device_id=plane_id(ss), device_id_type=MESH
            ).start()
        plane_sent.append(send)

    def plane_wait(buf, sem):
        some = buf.at[pl.ds(0, S - 1)]
        pltpu.make_async_copy(some, some, sem).wait()

    def landed(ref, sem):
        pltpu.make_async_copy(ref, ref, sem).wait()

    def take(key):
        pend.pop(key)()

    def home_wait(t, fn0):
        def fn():
            fn0()

        pl.when(period == t)(fn)

    def inj_wait():
        for xx in range(X):
            for kk in range(2):
                landed(inj_r.at[kk, :, lanes(xx)], inj_sem.at[xx * 2 + kk])

    barrier = pltpu.get_barrier_semaphore()
    def greet(device):
        pl.semaphore_signal(barrier, inc=1, device_id=device, device_id_type=MESH)

    for i in range(10):
        greet(plane_id(plane_spot(*OTHERS[i])))
    for dx in (2, 1, 3):
        for kk in range(2):
            greet(ring_id(lax.rem(x + dx, X), kk))
    for i in range(10, S - 1):
        greet(plane_id(plane_spot(*OTHERS[i])))
    greet(ring_id(x, 1 - core))

    for i in range(4):
        strip = pl.ds(pl.multiple_of(i * 512 + core * 256, 256), 256)
        pltpu.make_async_copy(sens.at[:, strip], sens_half.at[x_lo, :, pl.ds(i * 256, 256)], load_sem.at[0]).start()
    load_resid = pltpu.make_async_copy(resid.at[0], resid_v, load_sem.at[1])
    load_inv = pltpu.make_async_copy(inverse.at[0], inv_v, load_sem.at[2])
    load_act = pltpu.make_async_copy(active, act_v, load_sem.at[3])
    load_start = pltpu.make_async_copy(start, start_v, load_sem.at[4])
    load_ubus = pltpu.make_async_copy(unit_bus, ubus_v, load_sem.at[5])
    for load in (load_resid, load_inv, load_act, load_start, load_ubus):
        load.start()
    for source, stage, sem in ((gain, gain_s, load_sem.at[6]), (schur, schur_s, load_sem.at[7])):
        for kk in range(2):
            for i in range(4):
                pltpu.make_async_copy(
                    source.at[0, :, pl.ds(i * 512 + kk * 256, 256)], stage.at[kk, :, pl.ds(i * 256, 256)], sem
                ).start()

    pend['load_resid'] = load_resid.wait
    pend['load_inv'] = load_inv.wait
    pend['load_act'] = load_act.wait
    pend['load_start'] = load_start.wait
    pend['load_ubus'] = load_ubus.wait
    pend['gain_s'] = lambda: landed(gain_s, load_sem.at[6])
    pend['schur_s'] = lambda: landed(schur_s, load_sem.at[7])
    take('load_resid')
    take('load_inv')
    take('load_act')
    n = inv_v.shape[0]
    diagonal = lax.broadcasted_iota(jnp.int32, (n, n), 0) == lax.broadcasted_iota(jnp.int32, (n, n), 1)
    scale = 1.0 + 3.0 * act_v[...].astype(F32)
    scale = jnp.sum(jnp.where(diagonal, jnp.broadcast_to(scale, (n, n)), 0.0), axis=1, keepdims=True)
    weighted = resid_v[...] * scale
    weighted_v[...] = weighted
    solve_s[...] = dot(inv_v[...], weighted.astype(BF16)).astype(BF16)
    landed(sens_half.at[x_lo], load_sem.at[0])
    pl.semaphore_wait(barrier, 22)

    half = sens_half.shape[1] // 2
    for i, step in enumerate((1, X - 1)):
        rows = pl.ds(i * half, half)
        far_copy(
            sens_half.at[x_lo, rows], sens_half.at[x_lo, rows], sens_sem.at[i], lax.rem(x + step, X), core
        )

    def sens_wait():
        for i in range(2):
            rows = pl.ds(i * half, half)
            landed(sens_half.at[1 - x_lo, rows], sens_sem.at[i])

    pend['sens'] = sens_wait

    line = [(xx, kk) for xx in range(X) for kk in range(2)]
    send_solve = ring_group('solve', [
        (
            solve_s.at[kk * half : (kk + 1) * half, lanes(xx)],
            solve_r.at[x_lo, kk * half : (kk + 1) * half, lanes(period)],
            solve_sem.at[period * 2 + x_lo],
            xx,
            kk,
        )
        for xx, kk in line
    ])
    send_rhs = ring_group('rhs', [
        (rhs.at[0, :, lanes(xx)], rhs_r.at[period], rhs_sem.at[period], xx, x_lo) for xx in range(X)
    ])
    send_gain = ring_group('gain', [
        (gain_s.at[kk], gain_r.at[period, x_lo], gain_sem.at[period * 2 + x_lo], xx, kk) for xx, kk in line
    ])
    send_schur = ring_group('schur', [
        (schur_s.at[kk], schur_r.at[period, x_lo], schur_sem.at[period * 2 + x_lo], xx, kk) for xx, kk in line
    ])
    def half_solve(t, j, kk):
        return solve_r.at[j, pl.ds(pl.multiple_of(kk * half, 32), half), lanes(t)]

    def swap_solve(*periods):
        for t in periods:
            for j in range(2):
                take(f'solve{t}{j}')
                pend[f'swap{t}{j}'] = lambda t=t, j=j: landed(half_solve(t, j, 1 - core), swap_sem.at[t * 2 + j])
                far_copy(half_solve(t, j, core), half_solve(t, j, core), swap_sem.at[t * 2 + j], x, 1 - core)
        for t in periods:
            for j in range(2):
                take(f'swap{t}{j}')

    send_solve(3)

    for t in range(T):
        for j in range(2):
            pend[f'solve{t}{j}'] = lambda t=t, j=j: landed(half_solve(t, j, core), solve_sem.at[t * 2 + j])
    take('load_start')
    start_b[...] = start_v[...].astype(BF16)
    own = x_lo == core

    @pl.when(own)
    def _():
        state_g[0, spot] = start_b[:, lanes(x)]

    far_copy(start_b.at[:, lanes(x_pair)], state_g.at[0, spot], first_sem.at[0], x_pair, core, own)

    def first_wait():
        @pl.when(jnp.logical_not(own))
        def _():
            landed(state_g.at[0, spot], first_sem.at[0])

    pend['first'] = first_wait
    for t in range(T):
        pend[f'rhs{t}'] = lambda t=t: landed(rhs_r.at[t], rhs_sem.at[t])
    send_rhs(3)

    for t in range(T):
        for j in range(2):
            pend[f'gain{t}{j}'] = lambda t=t, j=j: landed(gain_r.at[t, j], gain_sem.at[t * 2 + j])
    take('first')
    pend['xg0'] = lambda: plane_wait(state_g.at[0], xg_sem.at[0])
    plane_copy(lambda ss: state_g.at[0, spot], state_g.at[0, spot], xg_sem.at[0])

    for t in range(T):
        for j in range(2):
            pend[f'schur{t}{j}'] = lambda t=t, j=j: landed(schur_r.at[t, j], schur_sem.at[t * 2 + j])
    take('load_ubus')
    for i in range(4):
        units = ubus_v[:, pl.ds(pl.multiple_of(i * 512 + core * 256, 256), 256)]
        for j in range(2):
            first = (z * 8 + j * 4 + y) * n
            ids = lax.broadcasted_iota(jnp.int32, (n, 256), 0) + first
            onehot[j * n : (j + 1) * n, i * 256 : (i + 1) * 256] = jnp.where(
                ids == jnp.broadcast_to(units, (n, 256)), 1.0, 0.0
            ).astype(BF16)

    sens_t[x_lo] = sens_half[x_lo].T
    take('gain_s')
    take('schur_s')
    send_solve(0, 1, 2)
    send_gain(1, 2)
    take('sens')
    sens_t[1 - x_lo] = sens_half[1 - x_lo].T
    swap_solve(3)

    def reduce_start(t, partial):
        pend[f'rs{t}'] = lambda: plane_wait(rs_r.at[t], rs_sem.at[t])
        rs_s[t] = partial.astype(BF16).reshape(S, 64, cols)
        plane_copy(lambda ss: rs_s.at[t, ss], rs_r.at[t, spot], rs_sem.at[t])
        rs_r[t, spot] = rs_s[t, spot]

    last = (T - 1) * cols
    reduce_start(T - 1, dot(sens_t[0], solve_r[0, :, last:]) + dot(sens_t[1], solve_r[1, :, last:]))
    send_rhs(0, 1, 2)
    swap_solve(0, 1, 2)
    part_v[...] = dot(sens_t[0], solve_r[0, :, :last]) + dot(sens_t[1], solve_r[1, :, :last])

    def send_cg(t):
        pend[f'cg{t}'] = lambda: plane_wait(cost_g.at[t], cg_sem.at[t])
        plane_copy(lambda ss: cost_g.at[t, spot], cost_g.at[t, spot], cg_sem.at[t])

    for t in reversed(range(T)):
        if t < T - 1:
            take(f'pair{t + 1}')
            reduce_start(
                t, part_v[:, t * cols : (t + 1) * cols] + dot(gain_t[t], cost_p[t + 1].reshape(2 * 64, cols))
            )
            if t == 2:
                send_gain(0, 3)
            elif t == 1:
                send_schur(0, 2)
            else:
                send_schur(1, 3)
        if t > 0:
            for j in range(2):
                take(f'gain{t - 1}{j}')
                gain_t[t - 1, :, j * 64 : (j + 1) * 64] = gain_r[t - 1, j].T
        take(f'rhs{t}')
        take(f'rs{t}')
        total = rhs_r[t] + jnp.sum(rs_r[t].astype(F32), axis=0)
        cost_v[t] = total
        rounded = total.astype(BF16)
        cost_g[t, spot] = rounded
        if t > 0:
            cost_p[t, core] = rounded
            pend[f'pair{t}'] = lambda t=t: landed(cost_p.at[t, 1 - core], pair_sem.at[t])
            far_copy(cost_g.at[t, spot], cost_p.at[t, core], pair_sem.at[t], x, 1 - core)
        else:
            send_cg(0)
            send_cg(1)
        pend[f'cout{t}'] = lambda t=t: home_wait(t, lambda: [landed(cost_out.at[0, :, lanes(xx)], cout_sem.at[xx]) for xx in range(X)])
        ring_copy(cost_v.at[t], cost_out.at[0, :, lanes(x)], cout_sem.at[x], 2 * (t // 2) + core, t % 2)

    for t in range(T):
        for j in range(2):
            if t == T - 1:
                take(f'gain{t}{j}')
            take(f'schur{t}{j}')
        width = S * 64
        if t == 0:
            take('xg0')
            moving = dot(gain_r[t].reshape(2 * 64, width), state_g[t].reshape(width, cols))
            take('cg0')
        else:
            take(f'cg{t}')
            pushed = dot(schur_r[t].reshape(2 * 64, width), cost_g[t].reshape(width, cols))
            take(f'xg{t}')
        if t == T - 1:
            moved = dot(onehot[...], state_g[t].reshape(width, cols))
            inj_s[t] = moved.astype(BF16).reshape(2, n, cols)
            for j in range(2):
                pend[f'inj{t}'] = lambda t=t: home_wait(t, inj_wait)
                ring_copy(
                    inj_s.at[t, j], inj_r.at[core, :, lanes(x)], inj_sem.at[x * 2 + core], 2 * (t // 2) + j, t % 2
                )
        if t == 0:
            pushed = dot(schur_r[t].reshape(2 * 64, width), cost_g[t].reshape(width, cols))
        else:
            moving = dot(gain_r[t].reshape(2 * 64, width), state_g[t].reshape(width, cols))
        full = moving - pushed
        full_v[t] = full.reshape(2, 64, cols)
        pend[f'full{t}'] = lambda t=t: landed(full_r.at[t], full_sem.at[t])
        far_copy(full_v.at[t, 1 - core], full_r.at[t], full_sem.at[t], x, 1 - core)
        take(f'full{t}')
        total = full_v[t, core] + full_r[t]
        state_v[t] = total
        if t < T - 1:
            state_g[t + 1, spot] = total.astype(BF16)
            pend[f'xg{t + 1}'] = lambda t=t: plane_wait(state_g.at[t + 1], xg_sem.at[t + 1])
            plane_copy(lambda ss, t=t: state_g.at[t + 1, spot], state_g.at[t + 1, spot], xg_sem.at[t + 1])
            if t + 2 < T:
                send_cg(t + 2)
        pend[f'sout{t}'] = lambda t=t: home_wait(t, lambda: [landed(stor_out.at[0, :, lanes(xx)], sout_sem.at[xx]) for xx in range(X)])
        ring_copy(state_v.at[t], stor_out.at[0, :, lanes(x)], sout_sem.at[x], 2 * (t // 2) + core, t % 2)
        if t < T - 1:
            moved = dot(onehot[...], state_g[t].reshape(width, cols))
            inj_s[t] = moved.astype(BF16).reshape(2, n, cols)
            for j in range(2):
                pend[f'inj{t}'] = lambda t=t: home_wait(t, inj_wait)
                ring_copy(
                    inj_s.at[t, j], inj_r.at[core, :, lanes(x)], inj_sem.at[x * 2 + core], 2 * (t // 2) + j, t % 2
                )

    for t in range(T):
        take(f'inj{t}')
    network = weighted_v[...] - (inj_r[0].astype(F32) + inj_r[1].astype(F32))
    network_v[...] = network.astype(BF16)
    store = pltpu.make_async_copy(network_v, network_out, load_sem.at[8])
    store.start()
    for t in range(T):
        take(f'cout{t}')
        take(f'sout{t}')
    store.wait()

    for key in list(pend):
        take(key)
    for on, copy, *more in sent:
        if more:
            if not more[0]:
                continue
            had = period == more[0][0]
            for p in more[0][1:]:
                had = had | (period == p)
            on = on & had
        if on is None:
            copy.wait_send()
        else:
            pl.when(on)(copy.wait_send)
    for send in plane_sent:
        plane_wait(rs_s.at[0], send)


def finish(stor, cost, network, inverse, stor_out, cost_out, upd_out, stor_v, cost_v, network_v, inv_v, upd_v, sem):
    pairs = ((network, network_v), (inverse, inv_v), (stor, stor_v), (cost, cost_v))
    loads = [pltpu.make_async_copy(src, dst, sem.at[i]) for i, (src, dst) in enumerate(pairs)]
    for load in loads:
        load.start()
    loads[0].wait()
    loads[1].wait()
    upd_v[0] = dot(inv_v[0], network_v[...])
    stores = [pltpu.make_async_copy(upd_v, upd_out, sem.at[4])]
    stores[0].start()
    for i, (src, dst) in enumerate(((stor_v, stor_out), (cost_v, cost_out))):
        loads[2 + i].wait()
        stores.append(pltpu.make_async_copy(src, dst, sem.at[5 + i]))
        stores[-1].start()
    for copy in stores:
        copy.wait()


def body(gain, schur, inverse_blocks, sensitivity, residual_bus, unit_rhs, start_state, active_set, unit_bus):
    anywhere = pl.BlockSpec(memory_space=pl.ANY)
    n = inverse_blocks.shape[1]
    dma = pltpu.SemaphoreType.DMA
    scratch = [
        pltpu.VMEM((2, n, 1024), BF16),
        pltpu.VMEM((2, 1024, n), BF16),
        pltpu.VMEM((n, 512), F32),
        pltpu.VMEM((n, n), BF16),
        pltpu.VMEM((1, n), jnp.int32),
        pltpu.VMEM((1, 2048), jnp.int32),
        pltpu.VMEM((64, 512), F32),
        pltpu.VMEM((64, 512), BF16),
        pltpu.VMEM((n, 512), F32),
        pltpu.VMEM((n, 512), BF16),
        pltpu.VMEM((2, n, 512), BF16),
        pltpu.VMEM((2, 64, 1024), BF16),
        pltpu.VMEM((2, 64, 1024), BF16),
        pltpu.VMEM((T, 2, 64, 1024), BF16),
        pltpu.VMEM((T, 2, 64, 1024), BF16),
        pltpu.VMEM((T - 1, 1024, 128), BF16),
        pltpu.VMEM((T, 64, 128), F32),
        pltpu.VMEM((1024, 384), F32),
        pltpu.VMEM((T, S, 64, 128), BF16),
        pltpu.VMEM((T, S, 64, 128), BF16),
        pltpu.VMEM((T, 64, 128), F32),
        pltpu.VMEM((T, S, 64, 128), BF16),
        pltpu.VMEM((T, 2, 64, 128), BF16),
        pltpu.VMEM((T, 64, 128), F32),
        pltpu.VMEM((T, S, 64, 128), BF16),
        pltpu.VMEM((T, 2, 64, 128), F32),
        pltpu.VMEM((T, 64, 128), F32),
        pltpu.VMEM((2 * n, 1024), BF16),
        pltpu.VMEM((T, 2, n, 128), BF16),
        pltpu.VMEM((2, n, 512), BF16),
        pltpu.VMEM((n, 512), BF16),
        dma((9,)),
        dma((2,)),
        dma((8,)),
        dma((8,)),
        dma((8,)),
        dma((8,)),
        dma((4,)),
        dma((1,)),
        dma((4,)),
        dma((4,)),
        dma((4,)),
        dma((4,)),
        dma((4,)),
        dma((8,)),
        dma((4,)),
        dma((4,)),
        dma((80,)),
        dma((12,)),
    ]
    moved = pl.pallas_call(
        kernel,
        out_shape=(
            jax.ShapeDtypeStruct((1, 64, 512), F32),
            jax.ShapeDtypeStruct((1, 64, 512), F32),
            jax.ShapeDtypeStruct((n, 512), BF16),
        ),
        in_specs=[anywhere] * 9,
        out_specs=(anywhere,) * 3,
        scratch_shapes=scratch,
        compiler_params=pltpu.CompilerParams(
            collective_id=0, has_side_effects=True, vmem_limit_bytes=60 * 1024 * 1024
        ),
    )(
        gain, schur, inverse_blocks, sensitivity, residual_bus, unit_rhs, start_state, active_set,
        unit_bus.reshape(1, -1),
    )
    return pl.pallas_call(
        finish,
        out_shape=(
            jax.ShapeDtypeStruct((1, 64, 512), F32),
            jax.ShapeDtypeStruct((1, 64, 512), F32),
            jax.ShapeDtypeStruct((1, n, 512), F32),
        ),
        in_specs=[anywhere] * 4,
        out_specs=(anywhere,) * 3,
        scratch_shapes=[
            pltpu.VMEM((1, 64, 512), F32),
            pltpu.VMEM((1, 64, 512), F32),
            pltpu.VMEM((n, 512), BF16),
            pltpu.VMEM((1, n, n), BF16),
            pltpu.VMEM((1, n, 512), F32),
            dma((7,)),
        ],
        compiler_params=pltpu.CompilerParams(vmem_limit_bytes=60 * 1024 * 1024),
    )(*moved, inverse_blocks)


def solution(mesh):
    placed = (
        P("period", "bus", None),
        P("period", "bus", None),
        P("period", "bus", None),
        P("bus", None),
        P("period", "bus", None),
        P("period", "bus", None),
        P("bus", None),
        P("period", "bus"),
        P(),
    )
    return jax.shard_map(
        body,
        mesh=mesh,
        in_specs=placed,
        out_specs=(P("period", "bus", None), P("period", "bus", None), P("period", "bus", None)),
        check_vma=False,
    )
```

```python
import jax
import jax.numpy as jnp
from jax import lax
from jax.experimental import pallas as pl
from jax.experimental.pallas import tpu as pltpu
from jax.sharding import PartitionSpec as P

MESH = pl.DeviceIdType.MESH
T = 4
X = 4
S = 16
F32 = jnp.float32
OTHERS = sorted(
    ((dz, dy) for dz in range(4) for dy in range(4) if dz or dy), key=lambda d: -min(d[0], 4 - d[0]) - min(d[1], 4 - d[1])
)
BF16 = jnp.bfloat16


def dot(a, b):
    return jnp.dot(a, b, preferred_element_type=F32)


def kernel(
    gain, schur, inverse, sens, resid, rhs, start, active, unit_bus,
    stor_out, cost_out, network_out,
    sens_half, sens_t, resid_v, inv_v, act_v, ubus_v, start_v, start_b, weighted_v, solve_s, solve_r,
    gain_s, schur_s, gain_r, schur_r, gain_t, rhs_r, part_v, rs_s, rs_r, cost_v, cost_g, cost_p,
    state_v, state_g, full_v, full_r, onehot, inj_s, inj_p, inj_r, network_v,
    load_sem, sens_sem, solve_sem, swap_sem, gain_sem, schur_sem, rhs_sem, first_sem, rs_sem, cg_sem, xg_sem, pair_sem, full_sem,
    inj_sem, injp_sem, cout_sem, sout_sem, send_ring, send_plane,
):
    period = lax.axis_index("period")
    bus = lax.axis_index("bus")
    x_hi, core = lax.div(period, 2), lax.rem(period, 2)
    z, x_lo, y = lax.div(bus, 8), lax.rem(lax.div(bus, 4), 2), lax.rem(bus, 4)
    x = 2 * x_hi + x_lo
    spot = z * 4 + y
    x_pair = x + 1 - 2 * x_lo
    cols = 128

    def ring_id(xx, kk):
        return (2 * lax.div(xx, 2) + kk, z * 8 + lax.rem(xx, 2) * 4 + y)

    def plane_id(ss):
        return (period, lax.div(ss, 4) * 8 + x_lo * 4 + lax.rem(ss, 4))

    def plane_spot(dz, dy):
        return lax.rem(z + dz, 4) * 4 + lax.rem(y + dy, 4)

    def lanes(xx):
        return pl.ds(pl.multiple_of(xx * cols, cols), cols)

    pend = {}
    started = set()
    sent = []

    def ring_copy(src, dst, recv, xx, kk):
        send = send_ring.at[len(sent)]
        mine = (x == xx) & (core == kk)
        remote = pltpu.make_async_remote_copy(
            src_ref=src, dst_ref=dst, send_sem=send, recv_sem=recv, device_id=ring_id(xx, kk), device_id_type=MESH
        )

        @pl.when(mine)
        def _():
            pltpu.make_async_copy(src, dst, recv).start()

        @pl.when(jnp.logical_not(mine))
        def _():
            remote.start()

        sent.append((jnp.logical_not(mine), remote))

    def ring_group(name, copies):
        made = []
        for src, dst, recv, xx, kk in copies:
            mine = (x == xx) & (core == kk)
            remote = pltpu.make_async_remote_copy(
                src_ref=src, dst_ref=dst, send_sem=send_ring.at[len(sent)], recv_sem=recv,
                device_id=ring_id(xx, kk), device_id_type=MESH,
            )
            made.append((mine, remote, pltpu.make_async_copy(src, dst, recv)))
            sent.append([jnp.logical_not(mine), remote, []])
        mark = sent[-len(made):]

        def start(*periods):
            for m in mark:
                m[2].extend(periods)
            for p in periods:
                started.add((name, p))
            on = period == periods[0]
            for p in periods[1:]:
                on = on | (period == p)
            @pl.when(on)
            def _():
                for mine, remote, local in made:
                    pl.when(mine)(local.start)
                    pl.when(jnp.logical_not(mine))(remote.start)

        return start

    def far_copy(src, dst, recv, xx, kk, on=None):
        send = send_ring.at[len(sent)]
        remote = pltpu.make_async_remote_copy(
            src_ref=src, dst_ref=dst, send_sem=send, recv_sem=recv, device_id=ring_id(xx, kk), device_id_type=MESH
        )
        if on is None:
            remote.start()
        else:
            pl.when(on)(remote.start)
        sent.append((on, remote))

    plane_sent = []

    def plane_copy(src_at, dst, recv):
        send = send_plane.at[len(plane_sent)]

        for dz, dy in OTHERS:
            ss = plane_spot(dz, dy)
            pltpu.make_async_remote_copy(
                src_ref=src_at(ss), dst_ref=dst, send_sem=send, recv_sem=recv, device_id=plane_id(ss), device_id_type=MESH
            ).start()
        plane_sent.append(send)

    def plane_wait(buf, sem):
        some = buf.at[pl.ds(0, S - 1)]
        pltpu.make_async_copy(some, some, sem).wait()

    def landed(ref, sem):
        pltpu.make_async_copy(ref, ref, sem).wait()

    def take(key):
        pend.pop(key)()

    def home_wait(t, fn0):
        def fn():
            fn0()

        pl.when(period == t)(fn)

    def inj_wait():
        for xx in range(X):
            landed(inj_r.at[:, lanes(xx)], inj_sem.at[xx])

    barrier = pltpu.get_barrier_semaphore()
    def greet(device):
        pl.semaphore_signal(barrier, inc=1, device_id=device, device_id_type=MESH)

    for i in range(10):
        greet(plane_id(plane_spot(*OTHERS[i])))
    for dx in (2, 1, 3):
        for kk in range(2):
            greet(ring_id(lax.rem(x + dx, X), kk))
    for i in range(10, S - 1):
        greet(plane_id(plane_spot(*OTHERS[i])))
    greet(ring_id(x, 1 - core))

    for i in range(4):
        strip = pl.ds(pl.multiple_of(i * 512 + core * 256, 256), 256)
        pltpu.make_async_copy(sens.at[:, strip], sens_half.at[x_lo, :, pl.ds(i * 256, 256)], load_sem.at[0]).start()
    load_resid = pltpu.make_async_copy(resid.at[0], resid_v, load_sem.at[1])
    load_inv = pltpu.make_async_copy(inverse.at[0], inv_v, load_sem.at[2])
    load_act = pltpu.make_async_copy(active, act_v, load_sem.at[3])
    load_start = pltpu.make_async_copy(start, start_v, load_sem.at[4])
    load_ubus = pltpu.make_async_copy(unit_bus, ubus_v, load_sem.at[5])
    for load in (load_resid, load_inv, load_act, load_start, load_ubus):
        load.start()
    for source, stage, sem in ((gain, gain_s, load_sem.at[6]), (schur, schur_s, load_sem.at[7])):
        for kk in range(2):
            for i in range(4):
                pltpu.make_async_copy(
                    source.at[0, :, pl.ds(i * 512 + kk * 256, 256)], stage.at[kk, :, pl.ds(i * 256, 256)], sem
                ).start()

    pend['load_resid'] = load_resid.wait
    pend['load_inv'] = load_inv.wait
    pend['load_act'] = load_act.wait
    pend['load_start'] = load_start.wait
    pend['load_ubus'] = load_ubus.wait
    pend['gain_s'] = lambda: landed(gain_s, load_sem.at[6])
    pend['schur_s'] = lambda: landed(schur_s, load_sem.at[7])
    take('load_resid')
    take('load_inv')
    take('load_act')
    n = inv_v.shape[0]
    diagonal = lax.broadcasted_iota(jnp.int32, (n, n), 0) == lax.broadcasted_iota(jnp.int32, (n, n), 1)
    scale = 1.0 + 3.0 * act_v[...].astype(F32)
    scale = jnp.sum(jnp.where(diagonal, jnp.broadcast_to(scale, (n, n)), 0.0), axis=1, keepdims=True)
    weighted = resid_v[...] * scale
    weighted_v[...] = weighted
    solve_s[...] = dot(inv_v[...], weighted.astype(BF16)).astype(BF16)
    landed(sens_half.at[x_lo], load_sem.at[0])
    pl.semaphore_wait(barrier, 22)

    half = sens_half.shape[1] // 2
    for i, step in enumerate((1, X - 1)):
        rows = pl.ds(i * half, half)
        far_copy(
            sens_half.at[x_lo, rows], sens_half.at[x_lo, rows], sens_sem.at[i], lax.rem(x + step, X), core
        )

    def sens_wait():
        for i in range(2):
            rows = pl.ds(i * half, half)
            landed(sens_half.at[1 - x_lo, rows], sens_sem.at[i])

    pend['sens'] = sens_wait

    line = [(xx, kk) for xx in range(X) for kk in range(2)]
    send_solve = ring_group('solve', [
        (
            solve_s.at[kk * half : (kk + 1) * half, lanes(xx)],
            solve_r.at[x_lo, kk * half : (kk + 1) * half, lanes(period)],
            solve_sem.at[period * 2 + x_lo],
            xx,
            kk,
        )
        for xx, kk in line
    ])
    send_rhs = ring_group('rhs', [
        (rhs.at[0, :, lanes(xx)], rhs_r.at[period], rhs_sem.at[period], xx, x_lo) for xx in range(X)
    ])
    send_gain = ring_group('gain', [
        (gain_s.at[kk], gain_r.at[period, x_lo], gain_sem.at[period * 2 + x_lo], xx, kk) for xx, kk in line
    ])
    send_schur = ring_group('schur', [
        (schur_s.at[kk], schur_r.at[period, x_lo], schur_sem.at[period * 2 + x_lo], xx, kk) for xx, kk in line
    ])
    def half_solve(t, j, kk):
        return solve_r.at[j, pl.ds(pl.multiple_of(kk * half, 32), half), lanes(t)]

    def swap_solve(*periods):
        for t in periods:
            for j in range(2):
                take(f'solve{t}{j}')
                pend[f'swap{t}{j}'] = lambda t=t, j=j: landed(half_solve(t, j, 1 - core), swap_sem.at[t * 2 + j])
                far_copy(half_solve(t, j, core), half_solve(t, j, core), swap_sem.at[t * 2 + j], x, 1 - core)
        for t in periods:
            for j in range(2):
                take(f'swap{t}{j}')

    send_solve(3)

    for t in range(T):
        for j in range(2):
            pend[f'solve{t}{j}'] = lambda t=t, j=j: landed(half_solve(t, j, core), solve_sem.at[t * 2 + j])
    take('load_start')
    start_b[...] = start_v[...].astype(BF16)
    own = x_lo == core

    @pl.when(own)
    def _():
        state_g[0, spot] = start_b[:, lanes(x)]

    far_copy(start_b.at[:, lanes(x_pair)], state_g.at[0, spot], first_sem.at[0], x_pair, core, own)

    def first_wait():
        @pl.when(jnp.logical_not(own))
        def _():
            landed(state_g.at[0, spot], first_sem.at[0])

    pend['first'] = first_wait
    for t in range(T):
        pend[f'rhs{t}'] = lambda t=t: landed(rhs_r.at[t], rhs_sem.at[t])
    send_rhs(3)

    for t in range(T):
        for j in range(2):
            pend[f'gain{t}{j}'] = lambda t=t, j=j: landed(gain_r.at[t, j], gain_sem.at[t * 2 + j])
    take('first')
    pend['xg0'] = lambda: plane_wait(state_g.at[0], xg_sem.at[0])
    plane_copy(lambda ss: state_g.at[0, spot], state_g.at[0, spot], xg_sem.at[0])

    for t in range(T):
        for j in range(2):
            pend[f'schur{t}{j}'] = lambda t=t, j=j: landed(schur_r.at[t, j], schur_sem.at[t * 2 + j])
    take('load_ubus')
    for i in range(4):
        units = ubus_v[:, pl.ds(pl.multiple_of(i * 512 + core * 256, 256), 256)]
        for j in range(2):
            first = (z * 8 + j * 4 + y) * n
            ids = lax.broadcasted_iota(jnp.int32, (n, 256), 0) + first
            onehot[j * n : (j + 1) * n, i * 256 : (i + 1) * 256] = jnp.where(
                ids == jnp.broadcast_to(units, (n, 256)), 1.0, 0.0
            ).astype(BF16)

    sens_t[x_lo] = sens_half[x_lo].T
    take('gain_s')
    take('schur_s')
    send_solve(0, 1, 2)
    send_gain(1, 2)
    take('sens')
    sens_t[1 - x_lo] = sens_half[1 - x_lo].T
    swap_solve(3)

    def reduce_start(t, partial):
        pend[f'rs{t}'] = lambda: plane_wait(rs_r.at[t], rs_sem.at[t])
        send = send_plane.at[len(plane_sent)]
        plane_sent.append(send)
        for dz in (2, 1, 3, 0):
            zz = lax.rem(z + dz, 4)
            block = partial(pl.ds(pl.multiple_of(zz * 256, 256), 256))
            rs_s[t, pl.ds(zz * 4, 4)] = block.astype(BF16).reshape(4, 64, cols)
            for dy in (2, 1, 3) if dz == 0 else (2, 1, 3, 0):
                ss = plane_spot(dz, dy)
                pltpu.make_async_remote_copy(
                    src_ref=rs_s.at[t, ss], dst_ref=rs_r.at[t, spot], send_sem=send, recv_sem=rs_sem.at[t],
                    device_id=plane_id(ss), device_id_type=MESH,
                ).start()
        rs_r[t, spot] = rs_s[t, spot]

    last = (T - 1) * cols
    reduce_start(
        T - 1, lambda rows: dot(sens_t[0, rows], solve_r[0, :, last:]) + dot(sens_t[1, rows], solve_r[1, :, last:])
    )
    send_rhs(0, 1, 2)
    swap_solve(0, 1, 2)
    part_v[...] = dot(sens_t[0], solve_r[0, :, :last]) + dot(sens_t[1], solve_r[1, :, :last])

    def send_cg(t):
        pend[f'cg{t}'] = lambda: plane_wait(cost_g.at[t], cg_sem.at[t])
        plane_copy(lambda ss: cost_g.at[t, spot], cost_g.at[t, spot], cg_sem.at[t])

    for t in reversed(range(T)):
        if t < T - 1:
            take(f'pair{t + 1}')
            reduce_start(
                t,
                lambda rows, t=t: part_v[rows, t * cols : (t + 1) * cols]
                + dot(gain_t[t, rows], cost_p[t + 1].reshape(2 * 64, cols)),
            )
            if t == 2:
                send_gain(0, 3)
            elif t == 1:
                send_schur(0, 2)
            else:
                send_schur(1, 3)
        if t > 0:
            for j in range(2):
                take(f'gain{t - 1}{j}')
                gain_t[t - 1, :, j * 64 : (j + 1) * 64] = gain_r[t - 1, j].T
        take(f'rhs{t}')
        take(f'rs{t}')
        total = rhs_r[t] + jnp.sum(rs_r[t].astype(F32), axis=0)
        cost_v[t] = total
        rounded = total.astype(BF16)
        cost_g[t, spot] = rounded
        if t > 0:
            cost_p[t, core] = rounded
            pend[f'pair{t}'] = lambda t=t: landed(cost_p.at[t, 1 - core], pair_sem.at[t])
            far_copy(cost_g.at[t, spot], cost_p.at[t, core], pair_sem.at[t], x, 1 - core)
        else:
            send_cg(0)
            send_cg(1)
        pend[f'cout{t}'] = lambda t=t: home_wait(t, lambda: [landed(cost_out.at[0, :, lanes(xx)], cout_sem.at[xx]) for xx in range(X)])
        ring_copy(cost_v.at[t], cost_out.at[0, :, lanes(x)], cout_sem.at[x], 2 * (t // 2) + core, t % 2)

    def inj_add(t):
        inj_s[t, 1 - core] = dot(
            onehot[pl.ds(pl.multiple_of((1 - core) * n, 64), n), :], state_g[t].reshape(S * 64, cols)
        ).astype(BF16)
        far_copy(inj_s.at[t, 1 - core], inj_p.at[t], injp_sem.at[t], x, 1 - core)
        mine = dot(onehot[pl.ds(pl.multiple_of(core * n, 64), n), :], state_g[t].reshape(S * 64, cols))
        landed(inj_p.at[t], injp_sem.at[t])
        inj_s[t, core] = (mine + inj_p[t].astype(F32)).astype(BF16)
        pend[f'inj{t}'] = lambda t=t: home_wait(t, inj_wait)
        ring_copy(inj_s.at[t, core], inj_r.at[:, lanes(x)], inj_sem.at[x], 2 * (t // 2) + core, t % 2)

    for t in range(T):
        for j in range(2):
            if t == T - 1:
                take(f'gain{t}{j}')
            take(f'schur{t}{j}')
        width = S * 64
        if t == 0:
            take('xg0')
            moving = dot(gain_r[t].reshape(2 * 64, width), state_g[t].reshape(width, cols))
            take('cg0')
        else:
            take(f'cg{t}')
            pushed = dot(schur_r[t].reshape(2 * 64, width), cost_g[t].reshape(width, cols))
            take(f'xg{t}')
        if t == T - 1:
            inj_add(t)
        if t == 0:
            pushed = dot(schur_r[t].reshape(2 * 64, width), cost_g[t].reshape(width, cols))
        else:
            moving = dot(gain_r[t].reshape(2 * 64, width), state_g[t].reshape(width, cols))
        full = moving - pushed
        full_v[t] = full.reshape(2, 64, cols)
        pend[f'full{t}'] = lambda t=t: landed(full_r.at[t], full_sem.at[t])
        far_copy(full_v.at[t, 1 - core], full_r.at[t], full_sem.at[t], x, 1 - core)
        take(f'full{t}')
        total = full_v[t, core] + full_r[t]
        state_v[t] = total
        if t < T - 1:
            state_g[t + 1, spot] = total.astype(BF16)
            pend[f'xg{t + 1}'] = lambda t=t: plane_wait(state_g.at[t + 1], xg_sem.at[t + 1])
            plane_copy(lambda ss, t=t: state_g.at[t + 1, spot], state_g.at[t + 1, spot], xg_sem.at[t + 1])
            if t + 2 < T:
                send_cg(t + 2)
        pend[f'sout{t}'] = lambda t=t: home_wait(t, lambda: [landed(stor_out.at[0, :, lanes(xx)], sout_sem.at[xx]) for xx in range(X)])
        ring_copy(state_v.at[t], stor_out.at[0, :, lanes(x)], sout_sem.at[x], 2 * (t // 2) + core, t % 2)
        if t < T - 1:
            inj_add(t)

    for t in range(T):
        take(f'inj{t}')
    network = weighted_v[...] - inj_r[...].astype(F32)
    network_v[...] = network.astype(BF16)
    store = pltpu.make_async_copy(network_v, network_out, load_sem.at[8])
    store.start()
    for t in range(T):
        take(f'cout{t}')
        take(f'sout{t}')
    store.wait()

    for key in list(pend):
        take(key)
    for on, copy, *more in sent:
        if more:
            if not more[0]:
                continue
            had = period == more[0][0]
            for p in more[0][1:]:
                had = had | (period == p)
            on = on & had
        if on is None:
            copy.wait_send()
        else:
            pl.when(on)(copy.wait_send)
    for send in plane_sent:
        plane_wait(rs_s.at[0], send)


def finish(stor, cost, network, inverse, stor_out, cost_out, upd_out, stor_v, cost_v, network_v, inv_v, upd_v, sem):
    pairs = ((network, network_v), (inverse, inv_v), (stor, stor_v), (cost, cost_v))
    loads = [pltpu.make_async_copy(src, dst, sem.at[i]) for i, (src, dst) in enumerate(pairs)]
    for load in loads:
        load.start()
    loads[0].wait()
    loads[1].wait()
    upd_v[0] = dot(inv_v[0], network_v[...])
    stores = [pltpu.make_async_copy(upd_v, upd_out, sem.at[4])]
    stores[0].start()
    for i, (src, dst) in enumerate(((stor_v, stor_out), (cost_v, cost_out))):
        loads[2 + i].wait()
        stores.append(pltpu.make_async_copy(src, dst, sem.at[5 + i]))
        stores[-1].start()
    for copy in stores:
        copy.wait()


def body(gain, schur, inverse_blocks, sensitivity, residual_bus, unit_rhs, start_state, active_set, unit_bus):
    anywhere = pl.BlockSpec(memory_space=pl.ANY)
    n = inverse_blocks.shape[1]
    dma = pltpu.SemaphoreType.DMA
    scratch = [
        pltpu.VMEM((2, n, 1024), BF16),
        pltpu.VMEM((2, 1024, n), BF16),
        pltpu.VMEM((n, 512), F32),
        pltpu.VMEM((n, n), BF16),
        pltpu.VMEM((1, n), jnp.int32),
        pltpu.VMEM((1, 2048), jnp.int32),
        pltpu.VMEM((64, 512), F32),
        pltpu.VMEM((64, 512), BF16),
        pltpu.VMEM((n, 512), F32),
        pltpu.VMEM((n, 512), BF16),
        pltpu.VMEM((2, n, 512), BF16),
        pltpu.VMEM((2, 64, 1024), BF16),
        pltpu.VMEM((2, 64, 1024), BF16),
        pltpu.VMEM((T, 2, 64, 1024), BF16),
        pltpu.VMEM((T, 2, 64, 1024), BF16),
        pltpu.VMEM((T - 1, 1024, 128), BF16),
        pltpu.VMEM((T, 64, 128), F32),
        pltpu.VMEM((1024, 384), F32),
        pltpu.VMEM((T, S, 64, 128), BF16),
        pltpu.VMEM((T, S, 64, 128), BF16),
        pltpu.VMEM((T, 64, 128), F32),
        pltpu.VMEM((T, S, 64, 128), BF16),
        pltpu.VMEM((T, 2, 64, 128), BF16),
        pltpu.VMEM((T, 64, 128), F32),
        pltpu.VMEM((T, S, 64, 128), BF16),
        pltpu.VMEM((T, 2, 64, 128), F32),
        pltpu.VMEM((T, 64, 128), F32),
        pltpu.VMEM((2 * n, 1024), BF16),
        pltpu.VMEM((T, 2, n, 128), BF16),
        pltpu.VMEM((T, n, 128), BF16),
        pltpu.VMEM((n, 512), BF16),
        pltpu.VMEM((n, 512), BF16),
        dma((9,)),
        dma((2,)),
        dma((8,)),
        dma((8,)),
        dma((8,)),
        dma((8,)),
        dma((4,)),
        dma((1,)),
        dma((4,)),
        dma((4,)),
        dma((4,)),
        dma((4,)),
        dma((4,)),
        dma((4,)),
        dma((4,)),
        dma((4,)),
        dma((4,)),
        dma((80,)),
        dma((12,)),
    ]
    moved = pl.pallas_call(
        kernel,
        out_shape=(
            jax.ShapeDtypeStruct((1, 64, 512), F32),
            jax.ShapeDtypeStruct((1, 64, 512), F32),
            jax.ShapeDtypeStruct((n, 512), BF16),
        ),
        in_specs=[anywhere] * 9,
        out_specs=(anywhere,) * 3,
        scratch_shapes=scratch,
        compiler_params=pltpu.CompilerParams(
            collective_id=0, has_side_effects=True, vmem_limit_bytes=60 * 1024 * 1024
        ),
    )(
        gain, schur, inverse_blocks, sensitivity, residual_bus, unit_rhs, start_state, active_set,
        unit_bus.reshape(1, -1),
    )
    return pl.pallas_call(
        finish,
        out_shape=(
            jax.ShapeDtypeStruct((1, 64, 512), F32),
            jax.ShapeDtypeStruct((1, 64, 512), F32),
            jax.ShapeDtypeStruct((1, n, 512), F32),
        ),
        in_specs=[anywhere] * 4,
        out_specs=(anywhere,) * 3,
        scratch_shapes=[
            pltpu.VMEM((1, 64, 512), F32),
            pltpu.VMEM((1, 64, 512), F32),
            pltpu.VMEM((n, 512), BF16),
            pltpu.VMEM((1, n, n), BF16),
            pltpu.VMEM((1, n, 512), F32),
            dma((7,)),
        ],
        compiler_params=pltpu.CompilerParams(vmem_limit_bytes=60 * 1024 * 1024),
    )(*moved, inverse_blocks)


def solution(mesh):
    placed = (
        P("period", "bus", None),
        P("period", "bus", None),
        P("period", "bus", None),
        P("bus", None),
        P("period", "bus", None),
        P("period", "bus", None),
        P("bus", None),
        P("period", "bus"),
        P(),
    )
    return jax.shard_map(
        body,
        mesh=mesh,
        in_specs=placed,
        out_specs=(P("period", "bus", None), P("period", "bus", None), P("period", "bus", None)),
        check_vma=False,
    )
```

```python
import jax
import jax.numpy as jnp
from jax import lax
from jax.experimental import pallas as pl
from jax.experimental.pallas import tpu as pltpu
from jax.sharding import PartitionSpec as P

MESH = pl.DeviceIdType.MESH
T = 4
X = 4
S = 16
F32 = jnp.float32
OTHERS = sorted(
    ((dz, dy) for dz in range(4) for dy in range(4) if dz or dy), key=lambda d: -min(d[0], 4 - d[0]) - min(d[1], 4 - d[1])
)
BF16 = jnp.bfloat16


def dot(a, b):
    return jnp.dot(a, b, preferred_element_type=F32)


def kernel(
    gain, schur, inverse, sens, resid, rhs, start, active, unit_bus,
    stor_out, cost_out, network_out,
    sens_half, sens_t, resid_v, inv_v, act_v, ubus_v, start_v, start_b, weighted_v, solve_s, solve_r,
    gain_s, schur_s, gain_r, schur_r, gain_t, rhs_r, part_v, rs_s, rs_r, cost_v, cost_g, cost_p,
    state_v, state_g, full_v, full_r, onehot, inj_s, inj_p, inj_r, network_v,
    load_sem, sens_sem, solve_sem, swap_sem, gain_sem, schur_sem, rhs_sem, first_sem, rs_sem, cg_sem, xg_sem, pair_sem, full_sem,
    inj_sem, injp_sem, cout_sem, sout_sem, send_ring, send_plane,
):
    period = lax.axis_index("period")
    bus = lax.axis_index("bus")
    x_hi, core = lax.div(period, 2), lax.rem(period, 2)
    z, x_lo, y = lax.div(bus, 8), lax.rem(lax.div(bus, 4), 2), lax.rem(bus, 4)
    x = 2 * x_hi + x_lo
    spot = z * 4 + y
    x_pair = x + 1 - 2 * x_lo
    cols = 128

    def ring_id(xx, kk):
        return (2 * lax.div(xx, 2) + kk, z * 8 + lax.rem(xx, 2) * 4 + y)

    def plane_id(ss):
        return (period, lax.div(ss, 4) * 8 + x_lo * 4 + lax.rem(ss, 4))

    def plane_spot(dz, dy):
        return lax.rem(z + dz, 4) * 4 + lax.rem(y + dy, 4)

    def lanes(xx):
        return pl.ds(pl.multiple_of(xx * cols, cols), cols)

    pend = {}
    started = set()
    sent = []

    def ring_copy(src, dst, recv, xx, kk):
        send = send_ring.at[len(sent)]
        mine = (x == xx) & (core == kk)
        remote = pltpu.make_async_remote_copy(
            src_ref=src, dst_ref=dst, send_sem=send, recv_sem=recv, device_id=ring_id(xx, kk), device_id_type=MESH
        )

        @pl.when(mine)
        def _():
            pltpu.make_async_copy(src, dst, recv).start()

        @pl.when(jnp.logical_not(mine))
        def _():
            remote.start()

        sent.append((jnp.logical_not(mine), remote))

    def ring_group(name, copies):
        made = []
        for src, dst, recv, xx, kk in copies:
            mine = (x == xx) & (core == kk)
            remote = pltpu.make_async_remote_copy(
                src_ref=src, dst_ref=dst, send_sem=send_ring.at[len(sent)], recv_sem=recv,
                device_id=ring_id(xx, kk), device_id_type=MESH,
            )
            made.append((mine, remote, pltpu.make_async_copy(src, dst, recv)))
            sent.append([jnp.logical_not(mine), remote, []])
        mark = sent[-len(made):]

        def start(*periods):
            for m in mark:
                m[2].extend(periods)
            for p in periods:
                started.add((name, p))
            on = period == periods[0]
            for p in periods[1:]:
                on = on | (period == p)
            @pl.when(on)
            def _():
                for mine, remote, local in made:
                    pl.when(mine)(local.start)
                    pl.when(jnp.logical_not(mine))(remote.start)

        return start

    def far_copy(src, dst, recv, xx, kk, on=None):
        send = send_ring.at[len(sent)]
        remote = pltpu.make_async_remote_copy(
            src_ref=src, dst_ref=dst, send_sem=send, recv_sem=recv, device_id=ring_id(xx, kk), device_id_type=MESH
        )
        if on is None:
            remote.start()
        else:
            pl.when(on)(remote.start)
        sent.append((on, remote))

    plane_sent = []

    def plane_copy(src_at, dst, recv):
        send = send_plane.at[len(plane_sent)]

        for dz, dy in OTHERS:
            ss = plane_spot(dz, dy)
            pltpu.make_async_remote_copy(
                src_ref=src_at(ss), dst_ref=dst, send_sem=send, recv_sem=recv, device_id=plane_id(ss), device_id_type=MESH
            ).start()
        plane_sent.append(send)

    def plane_wait(buf, sem):
        some = buf.at[pl.ds(0, S - 1)]
        pltpu.make_async_copy(some, some, sem).wait()

    def landed(ref, sem):
        pltpu.make_async_copy(ref, ref, sem).wait()

    def take(key):
        pend.pop(key)()

    def home_wait(t, fn0):
        def fn():
            fn0()

        pl.when(period == t)(fn)

    def inj_wait():
        for xx in range(X):
            landed(inj_r.at[:, lanes(xx)], inj_sem.at[xx])

    barrier = pltpu.get_barrier_semaphore()
    def greet(device):
        pl.semaphore_signal(barrier, inc=1, device_id=device, device_id_type=MESH)

    for i in range(10):
        greet(plane_id(plane_spot(*OTHERS[i])))
    for dx in (2, 1, 3):
        for kk in range(2):
            greet(ring_id(lax.rem(x + dx, X), kk))
    for i in range(10, S - 1):
        greet(plane_id(plane_spot(*OTHERS[i])))
    greet(ring_id(x, 1 - core))

    for i in range(4):
        strip = pl.ds(pl.multiple_of(i * 512 + core * 256, 256), 256)
        pltpu.make_async_copy(sens.at[:, strip], sens_half.at[x_lo, :, pl.ds(i * 256, 256)], load_sem.at[0]).start()
    load_resid = pltpu.make_async_copy(resid.at[0], resid_v, load_sem.at[1])
    load_inv = pltpu.make_async_copy(inverse.at[0], inv_v, load_sem.at[2])
    load_act = pltpu.make_async_copy(active, act_v, load_sem.at[3])
    load_start = pltpu.make_async_copy(start, start_v, load_sem.at[4])
    load_ubus = pltpu.make_async_copy(unit_bus, ubus_v, load_sem.at[5])
    for load in (load_resid, load_inv, load_act, load_start, load_ubus):
        load.start()
    for source, stage, sem in ((gain, gain_s, load_sem.at[6]), (schur, schur_s, load_sem.at[7])):
        for kk in range(2):
            for i in range(4):
                pltpu.make_async_copy(
                    source.at[0, :, pl.ds(i * 512 + kk * 256, 256)], stage.at[kk, :, pl.ds(i * 256, 256)], sem
                ).start()

    pend['load_resid'] = load_resid.wait
    pend['load_inv'] = load_inv.wait
    pend['load_act'] = load_act.wait
    pend['load_start'] = load_start.wait
    pend['load_ubus'] = load_ubus.wait
    pend['gain_s'] = lambda: landed(gain_s, load_sem.at[6])
    pend['schur_s'] = lambda: landed(schur_s, load_sem.at[7])
    take('load_resid')
    take('load_inv')
    take('load_act')
    n = inv_v.shape[0]
    diagonal = lax.broadcasted_iota(jnp.int32, (n, n), 0) == lax.broadcasted_iota(jnp.int32, (n, n), 1)
    scale = 1.0 + 3.0 * act_v[...].astype(F32)
    scale = jnp.sum(jnp.where(diagonal, jnp.broadcast_to(scale, (n, n)), 0.0), axis=1, keepdims=True)
    weighted = resid_v[...] * scale
    weighted_v[...] = weighted
    solve_s[...] = dot(inv_v[...], weighted.astype(BF16)).astype(BF16)
    landed(sens_half.at[x_lo], load_sem.at[0])
    pl.semaphore_wait(barrier, 22)

    half = sens_half.shape[1] // 2
    cut_row = 176
    pieces = (pl.ds(0, cut_row), pl.ds(cut_row, 2 * half - cut_row))
    for hi, rows in enumerate(pieces):
        for step in (1, X - 1):
            far_copy(
                sens_half.at[x_lo, rows], sens_half.at[x_lo, rows], sens_sem.at[hi], lax.rem(x + step, X), core,
                x_hi == hi,
            )

    def sens_wait():
        for hi, rows in enumerate(pieces):
            landed(sens_half.at[1 - x_lo, rows], sens_sem.at[hi])

    pend['sens'] = sens_wait

    line = [(xx, kk) for xx in range(X) for kk in range(2)]
    send_solve = ring_group('solve', [
        (
            solve_s.at[kk * half : (kk + 1) * half, lanes(xx)],
            solve_r.at[x_lo, kk * half : (kk + 1) * half, lanes(period)],
            solve_sem.at[period * 2 + x_lo],
            xx,
            kk,
        )
        for xx, kk in line
    ])
    send_rhs = ring_group('rhs', [
        (rhs.at[0, :, lanes(xx)], rhs_r.at[period], rhs_sem.at[period], xx, x_lo) for xx in range(X)
    ])
    send_gain = ring_group('gain', [
        (gain_s.at[kk], gain_r.at[period, x_lo], gain_sem.at[period * 2 + x_lo], xx, kk) for xx, kk in line
    ])
    send_schur = ring_group('schur', [
        (schur_s.at[kk], schur_r.at[period, x_lo], schur_sem.at[period * 2 + x_lo], xx, kk) for xx, kk in line
    ])
    def half_solve(t, j, kk):
        return solve_r.at[j, pl.ds(pl.multiple_of(kk * half, 32), half), lanes(t)]

    def swap_solve(*periods):
        for t in periods:
            for j in range(2):
                take(f'solve{t}{j}')
                pend[f'swap{t}{j}'] = lambda t=t, j=j: landed(half_solve(t, j, 1 - core), swap_sem.at[t * 2 + j])
                far_copy(half_solve(t, j, core), half_solve(t, j, core), swap_sem.at[t * 2 + j], x, 1 - core)
        for t in periods:
            for j in range(2):
                take(f'swap{t}{j}')

    send_solve(3)

    for t in range(T):
        for j in range(2):
            pend[f'solve{t}{j}'] = lambda t=t, j=j: landed(half_solve(t, j, core), solve_sem.at[t * 2 + j])
    take('load_start')
    start_b[...] = start_v[...].astype(BF16)
    own = x_lo == core

    @pl.when(own)
    def _():
        state_g[0, spot] = start_b[:, lanes(x)]

    far_copy(start_b.at[:, lanes(x_pair)], state_g.at[0, spot], first_sem.at[0], x_pair, core, own)

    def first_wait():
        @pl.when(jnp.logical_not(own))
        def _():
            landed(state_g.at[0, spot], first_sem.at[0])

    pend['first'] = first_wait
    for t in range(T):
        pend[f'rhs{t}'] = lambda t=t: landed(rhs_r.at[t], rhs_sem.at[t])
    send_rhs(3)

    for t in range(T):
        for j in range(2):
            pend[f'gain{t}{j}'] = lambda t=t, j=j: landed(gain_r.at[t, j], gain_sem.at[t * 2 + j])
    take('first')
    pend['xg0'] = lambda: plane_wait(state_g.at[0], xg_sem.at[0])
    plane_copy(lambda ss: state_g.at[0, spot], state_g.at[0, spot], xg_sem.at[0])

    for t in range(T):
        for j in range(2):
            pend[f'schur{t}{j}'] = lambda t=t, j=j: landed(schur_r.at[t, j], schur_sem.at[t * 2 + j])
    take('load_ubus')
    for i in range(4):
        units = ubus_v[:, pl.ds(pl.multiple_of(i * 512 + core * 256, 256), 256)]
        for j in range(2):
            first = (z * 8 + j * 4 + y) * n
            ids = lax.broadcasted_iota(jnp.int32, (n, 256), 0) + first
            onehot[j * n : (j + 1) * n, i * 256 : (i + 1) * 256] = jnp.where(
                ids == jnp.broadcast_to(units, (n, 256)), 1.0, 0.0
            ).astype(BF16)

    sens_t[x_lo] = sens_half[x_lo].T
    take('gain_s')
    take('schur_s')
    send_solve(0, 1, 2)
    send_gain(2)
    take('sens')
    sens_t[1 - x_lo] = sens_half[1 - x_lo].T
    swap_solve(3)

    def reduce_start(t, partial):
        pend[f'rs{t}'] = lambda: plane_wait(rs_r.at[t], rs_sem.at[t])
        send = send_plane.at[len(plane_sent)]
        plane_sent.append(send)
        for dz in (2, 1, 3, 0):
            zz = lax.rem(z + dz, 4)
            block = partial(pl.ds(pl.multiple_of(zz * 256, 256), 256))
            rs_s[t, pl.ds(zz * 4, 4)] = block.astype(BF16).reshape(4, 64, cols)
            for dy in (2, 1, 3) if dz == 0 else (2, 1, 3, 0):
                ss = plane_spot(dz, dy)
                pltpu.make_async_remote_copy(
                    src_ref=rs_s.at[t, ss], dst_ref=rs_r.at[t, spot], send_sem=send, recv_sem=rs_sem.at[t],
                    device_id=plane_id(ss), device_id_type=MESH,
                ).start()
        rs_r[t, spot] = rs_s[t, spot]

    last = (T - 1) * cols
    reduce_start(
        T - 1, lambda rows: dot(sens_t[0, rows], solve_r[0, :, last:]) + dot(sens_t[1, rows], solve_r[1, :, last:])
    )
    send_rhs(0, 1, 2)
    send_gain(1)
    swap_solve(0, 1, 2)
    part_v[...] = dot(sens_t[0], solve_r[0, :, :last]) + dot(sens_t[1], solve_r[1, :, :last])

    def send_cg(t):
        pend[f'cg{t}'] = lambda: plane_wait(cost_g.at[t], cg_sem.at[t])
        plane_copy(lambda ss: cost_g.at[t, spot], cost_g.at[t, spot], cg_sem.at[t])

    for t in reversed(range(T)):
        if t < T - 1:
            take(f'pair{t + 1}')
            reduce_start(
                t,
                lambda rows, t=t: part_v[rows, t * cols : (t + 1) * cols]
                + dot(gain_t[t, rows], cost_p[t + 1].reshape(2 * 64, cols)),
            )
            if t == 2:
                send_gain(0, 3)
            elif t == 1:
                send_schur(0, 2)
            else:
                send_schur(1, 3)
        if t > 0:
            for j in range(2):
                take(f'gain{t - 1}{j}')
                gain_t[t - 1, :, j * 64 : (j + 1) * 64] = gain_r[t - 1, j].T
        take(f'rhs{t}')
        take(f'rs{t}')
        total = rhs_r[t] + jnp.sum(rs_r[t].astype(F32), axis=0)
        cost_v[t] = total
        rounded = total.astype(BF16)
        cost_g[t, spot] = rounded
        if t > 0:
            cost_p[t, core] = rounded
            pend[f'pair{t}'] = lambda t=t: landed(cost_p.at[t, 1 - core], pair_sem.at[t])
            far_copy(cost_g.at[t, spot], cost_p.at[t, core], pair_sem.at[t], x, 1 - core)
        else:
            send_cg(0)
            send_cg(1)
        pend[f'cout{t}'] = lambda t=t: home_wait(t, lambda: [landed(cost_out.at[0, :, lanes(xx)], cout_sem.at[xx]) for xx in range(X)])
        ring_copy(cost_v.at[t], cost_out.at[0, :, lanes(x)], cout_sem.at[x], 2 * (t // 2) + core, t % 2)

    def inj_add(t):
        inj_s[t, 1 - core] = dot(
            onehot[pl.ds(pl.multiple_of((1 - core) * n, 64), n), :], state_g[t].reshape(S * 64, cols)
        ).astype(BF16)
        far_copy(inj_s.at[t, 1 - core], inj_p.at[t], injp_sem.at[t], x, 1 - core)
        mine = dot(onehot[pl.ds(pl.multiple_of(core * n, 64), n), :], state_g[t].reshape(S * 64, cols))
        landed(inj_p.at[t], injp_sem.at[t])
        inj_s[t, core] = (mine + inj_p[t].astype(F32)).astype(BF16)
        pend[f'inj{t}'] = lambda t=t: home_wait(t, inj_wait)
        ring_copy(inj_s.at[t, core], inj_r.at[:, lanes(x)], inj_sem.at[x], 2 * (t // 2) + core, t % 2)

    for t in range(T):
        for j in range(2):
            if t == T - 1:
                take(f'gain{t}{j}')
            take(f'schur{t}{j}')
        width = S * 64
        if t == 0:
            take('xg0')
            moving = dot(gain_r[t].reshape(2 * 64, width), state_g[t].reshape(width, cols))
            take('cg0')
        else:
            take(f'cg{t}')
            pushed = dot(schur_r[t].reshape(2 * 64, width), cost_g[t].reshape(width, cols))
            take(f'xg{t}')
        if t == T - 1:
            inj_add(t)
        if t == 0:
            pushed = dot(schur_r[t].reshape(2 * 64, width), cost_g[t].reshape(width, cols))
        else:
            moving = dot(gain_r[t].reshape(2 * 64, width), state_g[t].reshape(width, cols))
        full = moving - pushed
        full_v[t] = full.reshape(2, 64, cols)
        pend[f'full{t}'] = lambda t=t: landed(full_r.at[t], full_sem.at[t])
        far_copy(full_v.at[t, 1 - core], full_r.at[t], full_sem.at[t], x, 1 - core)
        take(f'full{t}')
        total = full_v[t, core] + full_r[t]
        state_v[t] = total
        if t < T - 1:
            state_g[t + 1, spot] = total.astype(BF16)
            pend[f'xg{t + 1}'] = lambda t=t: plane_wait(state_g.at[t + 1], xg_sem.at[t + 1])
            plane_copy(lambda ss, t=t: state_g.at[t + 1, spot], state_g.at[t + 1, spot], xg_sem.at[t + 1])
            if t + 2 < T:
                send_cg(t + 2)
        pend[f'sout{t}'] = lambda t=t: home_wait(t, lambda: [landed(stor_out.at[0, :, lanes(xx)], sout_sem.at[xx]) for xx in range(X)])
        ring_copy(state_v.at[t], stor_out.at[0, :, lanes(x)], sout_sem.at[x], 2 * (t // 2) + core, t % 2)
        if t < T - 1:
            inj_add(t)

    for t in range(T):
        take(f'inj{t}')
    network = weighted_v[...] - inj_r[...].astype(F32)
    network_v[...] = network.astype(BF16)
    store = pltpu.make_async_copy(network_v, network_out, load_sem.at[8])
    store.start()
    for t in range(T):
        take(f'cout{t}')
        take(f'sout{t}')
    store.wait()

    for key in list(pend):
        take(key)
    for on, copy, *more in sent:
        if more:
            if not more[0]:
                continue
            had = period == more[0][0]
            for p in more[0][1:]:
                had = had | (period == p)
            on = on & had
        if on is None:
            copy.wait_send()
        else:
            pl.when(on)(copy.wait_send)
    for send in plane_sent:
        plane_wait(rs_s.at[0], send)


def finish(stor, cost, network, inverse, stor_out, cost_out, upd_out, stor_v, cost_v, network_v, inv_v, upd_v, sem):
    pairs = ((network, network_v), (inverse, inv_v), (stor, stor_v), (cost, cost_v))
    loads = [pltpu.make_async_copy(src, dst, sem.at[i]) for i, (src, dst) in enumerate(pairs)]
    for load in loads:
        load.start()
    loads[0].wait()
    loads[1].wait()
    upd_v[0] = dot(inv_v[0], network_v[...])
    stores = [pltpu.make_async_copy(upd_v, upd_out, sem.at[4])]
    stores[0].start()
    for i, (src, dst) in enumerate(((stor_v, stor_out), (cost_v, cost_out))):
        loads[2 + i].wait()
        stores.append(pltpu.make_async_copy(src, dst, sem.at[5 + i]))
        stores[-1].start()
    for copy in stores:
        copy.wait()


def body(gain, schur, inverse_blocks, sensitivity, residual_bus, unit_rhs, start_state, active_set, unit_bus):
    anywhere = pl.BlockSpec(memory_space=pl.ANY)
    n = inverse_blocks.shape[1]
    dma = pltpu.SemaphoreType.DMA
    scratch = [
        pltpu.VMEM((2, n, 1024), BF16),
        pltpu.VMEM((2, 1024, n), BF16),
        pltpu.VMEM((n, 512), F32),
        pltpu.VMEM((n, n), BF16),
        pltpu.VMEM((1, n), jnp.int32),
        pltpu.VMEM((1, 2048), jnp.int32),
        pltpu.VMEM((64, 512), F32),
        pltpu.VMEM((64, 512), BF16),
        pltpu.VMEM((n, 512), F32),
        pltpu.VMEM((n, 512), BF16),
        pltpu.VMEM((2, n, 512), BF16),
        pltpu.VMEM((2, 64, 1024), BF16),
        pltpu.VMEM((2, 64, 1024), BF16),
        pltpu.VMEM((T, 2, 64, 1024), BF16),
        pltpu.VMEM((T, 2, 64, 1024), BF16),
        pltpu.VMEM((T - 1, 1024, 128), BF16),
        pltpu.VMEM((T, 64, 128), F32),
        pltpu.VMEM((1024, 384), F32),
        pltpu.VMEM((T, S, 64, 128), BF16),
        pltpu.VMEM((T, S, 64, 128), BF16),
        pltpu.VMEM((T, 64, 128), F32),
        pltpu.VMEM((T, S, 64, 128), BF16),
        pltpu.VMEM((T, 2, 64, 128), BF16),
        pltpu.VMEM((T, 64, 128), F32),
        pltpu.VMEM((T, S, 64, 128), BF16),
        pltpu.VMEM((T, 2, 64, 128), F32),
        pltpu.VMEM((T, 64, 128), F32),
        pltpu.VMEM((2 * n, 1024), BF16),
        pltpu.VMEM((T, 2, n, 128), BF16),
        pltpu.VMEM((T, n, 128), BF16),
        pltpu.VMEM((n, 512), BF16),
        pltpu.VMEM((n, 512), BF16),
        dma((9,)),
        dma((2,)),
        dma((8,)),
        dma((8,)),
        dma((8,)),
        dma((8,)),
        dma((4,)),
        dma((1,)),
        dma((4,)),
        dma((4,)),
        dma((4,)),
        dma((4,)),
        dma((4,)),
        dma((4,)),
        dma((4,)),
        dma((4,)),
        dma((4,)),
        dma((80,)),
        dma((12,)),
    ]
    moved = pl.pallas_call(
        kernel,
        out_shape=(
            jax.ShapeDtypeStruct((1, 64, 512), F32),
            jax.ShapeDtypeStruct((1, 64, 512), F32),
            jax.ShapeDtypeStruct((n, 512), BF16),
        ),
        in_specs=[anywhere] * 9,
        out_specs=(anywhere,) * 3,
        scratch_shapes=scratch,
        compiler_params=pltpu.CompilerParams(
            collective_id=0, has_side_effects=True, vmem_limit_bytes=60 * 1024 * 1024
        ),
    )(
        gain, schur, inverse_blocks, sensitivity, residual_bus, unit_rhs, start_state, active_set,
        unit_bus.reshape(1, -1),
    )
    return pl.pallas_call(
        finish,
        out_shape=(
            jax.ShapeDtypeStruct((1, 64, 512), F32),
            jax.ShapeDtypeStruct((1, 64, 512), F32),
            jax.ShapeDtypeStruct((1, n, 512), F32),
        ),
        in_specs=[anywhere] * 4,
        out_specs=(anywhere,) * 3,
        scratch_shapes=[
            pltpu.VMEM((1, 64, 512), F32),
            pltpu.VMEM((1, 64, 512), F32),
            pltpu.VMEM((n, 512), BF16),
            pltpu.VMEM((1, n, n), BF16),
            pltpu.VMEM((1, n, 512), F32),
            dma((7,)),
        ],
        compiler_params=pltpu.CompilerParams(vmem_limit_bytes=60 * 1024 * 1024),
    )(*moved, inverse_blocks)


def solution(mesh):
    placed = (
        P("period", "bus", None),
        P("period", "bus", None),
        P("period", "bus", None),
        P("bus", None),
        P("period", "bus", None),
        P("period", "bus", None),
        P("bus", None),
        P("period", "bus"),
        P(),
    )
    return jax.shard_map(
        body,
        mesh=mesh,
        in_specs=placed,
        out_specs=(P("period", "bus", None), P("period", "bus", None), P("period", "bus", None)),
        check_vma=False,
    )
```

```python
import jax
import jax.numpy as jnp
from jax import lax
from jax.experimental import pallas as pl
from jax.experimental.pallas import tpu as pltpu
from jax.sharding import PartitionSpec as P

MESH = pl.DeviceIdType.MESH
T = 4
X = 4
S = 16
F32 = jnp.float32
OTHERS = sorted(
    ((dz, dy) for dz in range(4) for dy in range(4) if dz or dy), key=lambda d: -min(d[0], 4 - d[0]) - min(d[1], 4 - d[1])
)
BF16 = jnp.bfloat16


def dot(a, b):
    return jnp.dot(a, b, preferred_element_type=F32)


def kernel(
    gain, schur, inverse, sens, resid, rhs, start, active, unit_bus,
    stor_out, cost_out, network_out,
    sens_half, sens_t, resid_v, inv_v, act_v, ubus_v, start_v, start_b, weighted_v, solve_s, solve_r,
    gain_s, schur_s, gain_r, schur_r, gain_t, rhs_r, part_v, rs_s, rs_r, cost_v, cost_g, cost_p,
    state_v, state_g, full_v, full_r, onehot, inj_s, inj_p, inj_r, network_v,
    load_sem, sens_sem, solve_sem, swap_sem, gain_sem, schur_sem, rhs_sem, first_sem, rs_sem, cg_sem, xg_sem, pair_sem, full_sem,
    inj_sem, injp_sem, cout_sem, sout_sem, send_ring, send_plane,
):
    period = lax.axis_index("period")
    bus = lax.axis_index("bus")
    x_hi, core = lax.div(period, 2), lax.rem(period, 2)
    z, x_lo, y = lax.div(bus, 8), lax.rem(lax.div(bus, 4), 2), lax.rem(bus, 4)
    x = 2 * x_hi + x_lo
    spot = z * 4 + y
    x_pair = x + 1 - 2 * x_lo
    cols = 128

    def ring_id(xx, kk):
        return (2 * lax.div(xx, 2) + kk, z * 8 + lax.rem(xx, 2) * 4 + y)

    def plane_id(ss):
        return (period, lax.div(ss, 4) * 8 + x_lo * 4 + lax.rem(ss, 4))

    def plane_spot(dz, dy):
        return lax.rem(z + dz, 4) * 4 + lax.rem(y + dy, 4)

    def lanes(xx):
        return pl.ds(pl.multiple_of(xx * cols, cols), cols)

    pend = {}
    started = set()
    sent = []

    def ring_copy(src, dst, recv, xx, kk):
        send = send_ring.at[len(sent)]
        mine = (x == xx) & (core == kk)
        remote = pltpu.make_async_remote_copy(
            src_ref=src, dst_ref=dst, send_sem=send, recv_sem=recv, device_id=ring_id(xx, kk), device_id_type=MESH
        )

        @pl.when(mine)
        def _():
            pltpu.make_async_copy(src, dst, recv).start()

        @pl.when(jnp.logical_not(mine))
        def _():
            remote.start()

        sent.append((jnp.logical_not(mine), remote))

    def ring_group(name, copies):
        made = []
        for src, dst, recv, xx, kk in copies:
            mine = (x == xx) & (core == kk)
            remote = pltpu.make_async_remote_copy(
                src_ref=src, dst_ref=dst, send_sem=send_ring.at[len(sent)], recv_sem=recv,
                device_id=ring_id(xx, kk), device_id_type=MESH,
            )
            made.append((mine, remote, pltpu.make_async_copy(src, dst, recv)))
            sent.append([jnp.logical_not(mine), remote, []])
        mark = sent[-len(made):]

        def start(*periods):
            for m in mark:
                m[2].extend(periods)
            for p in periods:
                started.add((name, p))
            on = period == periods[0]
            for p in periods[1:]:
                on = on | (period == p)
            @pl.when(on)
            def _():
                for mine, remote, local in made:
                    pl.when(mine)(local.start)
                    pl.when(jnp.logical_not(mine))(remote.start)

        return start

    def far_copy(src, dst, recv, xx, kk, on=None):
        send = send_ring.at[len(sent)]
        remote = pltpu.make_async_remote_copy(
            src_ref=src, dst_ref=dst, send_sem=send, recv_sem=recv, device_id=ring_id(xx, kk), device_id_type=MESH
        )
        if on is None:
            remote.start()
        else:
            pl.when(on)(remote.start)
        sent.append((on, remote))

    plane_sent = []

    def plane_copy(src_at, dst, recv):
        send = send_plane.at[len(plane_sent)]

        for dz, dy in OTHERS:
            ss = plane_spot(dz, dy)
            pltpu.make_async_remote_copy(
                src_ref=src_at(ss), dst_ref=dst, send_sem=send, recv_sem=recv, device_id=plane_id(ss), device_id_type=MESH
            ).start()
        plane_sent.append(send)

    def plane_wait(buf, sem):
        some = buf.at[pl.ds(0, S - 1)]
        pltpu.make_async_copy(some, some, sem).wait()

    def landed(ref, sem):
        pltpu.make_async_copy(ref, ref, sem).wait()

    def take(key):
        pend.pop(key)()

    def home_wait(t, fn0):
        def fn():
            fn0()

        pl.when(period == t)(fn)

    def inj_wait():
        for xx in range(X):
            landed(inj_r.at[:, lanes(xx)], inj_sem.at[xx])

    barrier = pltpu.get_barrier_semaphore()
    def greet(device):
        pl.semaphore_signal(barrier, inc=1, device_id=device, device_id_type=MESH)

    for i in range(10):
        greet(plane_id(plane_spot(*OTHERS[i])))
    for dx in (2, 1, 3):
        for kk in range(2):
            greet(ring_id(lax.rem(x + dx, X), kk))
    for i in range(10, S - 1):
        greet(plane_id(plane_spot(*OTHERS[i])))
    greet(ring_id(x, 1 - core))

    for i in range(4):
        strip = pl.ds(pl.multiple_of(i * 512 + core * 256, 256), 256)
        pltpu.make_async_copy(sens.at[:, strip], sens_half.at[x_lo, :, pl.ds(i * 256, 256)], load_sem.at[0]).start()
    load_resid = pltpu.make_async_copy(resid.at[0], resid_v, load_sem.at[1])
    load_inv = pltpu.make_async_copy(inverse.at[0], inv_v, load_sem.at[2])
    load_act = pltpu.make_async_copy(active, act_v, load_sem.at[3])
    load_start = pltpu.make_async_copy(start, start_v, load_sem.at[4])
    load_ubus = pltpu.make_async_copy(unit_bus, ubus_v, load_sem.at[5])
    for load in (load_resid, load_inv, load_act, load_start, load_ubus):
        load.start()
    for source, stage, sem in ((gain, gain_s, load_sem.at[6]), (schur, schur_s, load_sem.at[7])):
        for kk in range(2):
            for i in range(4):
                pltpu.make_async_copy(
                    source.at[0, :, pl.ds(i * 512 + kk * 256, 256)], stage.at[kk, :, pl.ds(i * 256, 256)], sem
                ).start()

    pend['load_resid'] = load_resid.wait
    pend['load_inv'] = load_inv.wait
    pend['load_act'] = load_act.wait
    pend['load_start'] = load_start.wait
    pend['load_ubus'] = load_ubus.wait
    pend['gain_s'] = lambda: landed(gain_s, load_sem.at[6])
    pend['schur_s'] = lambda: landed(schur_s, load_sem.at[7])
    take('load_resid')
    take('load_inv')
    take('load_act')
    n = inv_v.shape[0]
    diagonal = lax.broadcasted_iota(jnp.int32, (n, n), 0) == lax.broadcasted_iota(jnp.int32, (n, n), 1)
    scale = 1.0 + 3.0 * act_v[...].astype(F32)
    scale = jnp.sum(jnp.where(diagonal, jnp.broadcast_to(scale, (n, n)), 0.0), axis=1, keepdims=True)
    weighted = resid_v[...] * scale
    weighted_v[...] = weighted
    solve_s[...] = dot(inv_v[...], weighted.astype(BF16)).astype(BF16)
    landed(sens_half.at[x_lo], load_sem.at[0])
    pl.semaphore_wait(barrier, 22)

    half = sens_half.shape[1] // 2
    cut_row = 176
    pieces = (pl.ds(0, cut_row), pl.ds(cut_row, 2 * half - cut_row))
    for hi, rows in enumerate(pieces):
        for step in (1, X - 1):
            far_copy(
                sens_half.at[x_lo, rows], sens_half.at[x_lo, rows], sens_sem.at[hi], lax.rem(x + step, X), core,
                x_hi == hi,
            )

    def sens_wait():
        for hi, rows in enumerate(pieces):
            landed(sens_half.at[1 - x_lo, rows], sens_sem.at[hi])

    pend['sens'] = sens_wait

    line = [(xx, kk) for xx in range(X) for kk in range(2)]
    send_solve = ring_group('solve', [
        (
            solve_s.at[kk * half : (kk + 1) * half, lanes(xx)],
            solve_r.at[x_lo, kk * half : (kk + 1) * half, lanes(period)],
            solve_sem.at[period * 2 + x_lo],
            xx,
            kk,
        )
        for xx, kk in line
    ])
    send_rhs = ring_group('rhs', [
        (rhs.at[0, :, lanes(xx)], rhs_r.at[period], rhs_sem.at[period], xx, x_lo) for xx in range(X)
    ])
    send_gain = ring_group('gain', [
        (gain_s.at[kk], gain_r.at[period, x_lo], gain_sem.at[period * 2 + x_lo], xx, kk) for xx, kk in line
    ])
    send_schur = ring_group('schur', [
        (schur_s.at[kk], schur_r.at[period, x_lo], schur_sem.at[period * 2 + x_lo], xx, kk) for xx, kk in line
    ])
    def half_solve(t, j, kk):
        return solve_r.at[j, pl.ds(pl.multiple_of(kk * half, 32), half), lanes(t)]

    def swap_solve(*periods):
        for t in periods:
            for j in range(2):
                take(f'solve{t}{j}')
                pend[f'swap{t}{j}'] = lambda t=t, j=j: landed(half_solve(t, j, 1 - core), swap_sem.at[t * 2 + j])
                far_copy(half_solve(t, j, core), half_solve(t, j, core), swap_sem.at[t * 2 + j], x, 1 - core)
        for t in periods:
            for j in range(2):
                take(f'swap{t}{j}')

    send_solve(3)

    for t in range(T):
        for j in range(2):
            pend[f'solve{t}{j}'] = lambda t=t, j=j: landed(half_solve(t, j, core), solve_sem.at[t * 2 + j])
    take('load_start')
    start_b[...] = start_v[...].astype(BF16)
    own = x_lo == core

    @pl.when(own)
    def _():
        state_g[0, spot] = start_b[:, lanes(x)]

    far_copy(start_b.at[:, lanes(x_pair)], state_g.at[0, spot], first_sem.at[0], x_pair, core, own)

    def first_wait():
        @pl.when(jnp.logical_not(own))
        def _():
            landed(state_g.at[0, spot], first_sem.at[0])

    pend['first'] = first_wait
    for t in range(T):
        pend[f'rhs{t}'] = lambda t=t: landed(rhs_r.at[t], rhs_sem.at[t])
    send_rhs(3)

    for t in range(T):
        for j in range(2):
            pend[f'gain{t}{j}'] = lambda t=t, j=j: landed(gain_r.at[t, j], gain_sem.at[t * 2 + j])
    take('first')
    pend['xg0'] = lambda: plane_wait(state_g.at[0], xg_sem.at[0])
    plane_copy(lambda ss: state_g.at[0, spot], state_g.at[0, spot], xg_sem.at[0])

    for t in range(T):
        for j in range(2):
            pend[f'schur{t}{j}'] = lambda t=t, j=j: landed(schur_r.at[t, j], schur_sem.at[t * 2 + j])
    take('load_ubus')
    for i in range(4):
        units = ubus_v[:, pl.ds(pl.multiple_of(i * 512 + core * 256, 256), 256)]
        for j in range(2):
            first = (z * 8 + j * 4 + y) * n
            ids = lax.broadcasted_iota(jnp.int32, (n, 256), 0) + first
            onehot[j * n : (j + 1) * n, i * 256 : (i + 1) * 256] = jnp.where(
                ids == jnp.broadcast_to(units, (n, 256)), 1.0, 0.0
            ).astype(BF16)

    sens_t[x_lo] = sens_half[x_lo].T
    take('gain_s')
    take('schur_s')
    send_solve(0, 1, 2)
    send_gain(2)
    take('sens')
    sens_t[1 - x_lo] = sens_half[1 - x_lo].T
    swap_solve(3)

    def reduce_start(t, partial):
        pend[f'rs{t}'] = lambda: plane_wait(rs_r.at[t], rs_sem.at[t])
        send = send_plane.at[len(plane_sent)]
        plane_sent.append(send)
        for dz in (2, 1, 3, 0):
            zz = lax.rem(z + dz, 4)
            block = partial(pl.ds(pl.multiple_of(zz * 256, 256), 256))
            rs_s[t, pl.ds(zz * 4, 4)] = block.astype(BF16).reshape(4, 64, cols)
            for dy in (2, 1, 3) if dz == 0 else (2, 1, 3, 0):
                ss = plane_spot(dz, dy)
                pltpu.make_async_remote_copy(
                    src_ref=rs_s.at[t, ss], dst_ref=rs_r.at[t, spot], send_sem=send, recv_sem=rs_sem.at[t],
                    device_id=plane_id(ss), device_id_type=MESH,
                ).start()
        rs_r[t, spot] = rs_s[t, spot]

    last = (T - 1) * cols
    reduce_start(
        T - 1, lambda rows: dot(sens_t[0, rows], solve_r[0, :, last:]) + dot(sens_t[1, rows], solve_r[1, :, last:])
    )
    send_rhs(0, 1, 2)
    send_gain(1)
    swap_solve(0, 1, 2)
    part_v[...] = dot(sens_t[0], solve_r[0, :, :last]) + dot(sens_t[1], solve_r[1, :, :last])

    def send_cg(t):
        pend[f'cg{t}'] = lambda: plane_wait(cost_g.at[t], cg_sem.at[t])
        plane_copy(lambda ss: cost_g.at[t, spot], cost_g.at[t, spot], cg_sem.at[t])

    for t in reversed(range(T)):
        if t < T - 1:
            take(f'pair{t + 1}')
            reduce_start(
                t,
                lambda rows, t=t: part_v[rows, t * cols : (t + 1) * cols]
                + dot(gain_t[t, rows], cost_p[t + 1].reshape(2 * 64, cols)),
            )
            if t == 2:
                send_gain(0, 3)
            elif t == 1:
                send_schur(0, 2)
            else:
                send_schur(1, 3)
        if t > 0:
            for j in range(2):
                take(f'gain{t - 1}{j}')
                gain_t[t - 1, :, j * 64 : (j + 1) * 64] = gain_r[t - 1, j].T
        take(f'rhs{t}')
        take(f'rs{t}')
        total = rhs_r[t] + jnp.sum(rs_r[t].astype(F32), axis=0)
        cost_v[t] = total
        rounded = total.astype(BF16)
        cost_g[t, spot] = rounded
        if t > 0:
            cost_p[t, core] = rounded
            pend[f'pair{t}'] = lambda t=t: landed(cost_p.at[t, 1 - core], pair_sem.at[t])
            far_copy(cost_g.at[t, spot], cost_p.at[t, core], pair_sem.at[t], x, 1 - core)
        else:
            send_cg(0)
            send_cg(1)
        pend[f'cout{t}'] = lambda t=t: home_wait(t, lambda: [landed(cost_out.at[0, :, lanes(xx)], cout_sem.at[xx]) for xx in range(X)])
        ring_copy(cost_v.at[t], cost_out.at[0, :, lanes(x)], cout_sem.at[x], 2 * (t // 2) + core, t % 2)

    def inj_add(t):
        inj_s[t, 1 - core] = dot(
            onehot[pl.ds(pl.multiple_of((1 - core) * n, 64), n), :], state_g[t].reshape(S * 64, cols)
        ).astype(BF16)
        far_copy(inj_s.at[t, 1 - core], inj_p.at[t], injp_sem.at[t], x, 1 - core)
    def inj_end(t):
        mine = dot(onehot[pl.ds(pl.multiple_of(core * n, 64), n), :], state_g[t].reshape(S * 64, cols))
        landed(inj_p.at[t], injp_sem.at[t])
        inj_s[t, core] = (mine + inj_p[t].astype(F32)).astype(BF16)
        pend[f'inj{t}'] = lambda t=t: home_wait(t, inj_wait)
        ring_copy(inj_s.at[t, core], inj_r.at[:, lanes(x)], inj_sem.at[x], 2 * (t // 2) + core, t % 2)

    for t in range(T):
        for j in range(2):
            if t == T - 1:
                take(f'gain{t}{j}')
            take(f'schur{t}{j}')
        width = S * 64
        if t == 0:
            take('xg0')
            moving = dot(gain_r[t].reshape(2 * 64, width), state_g[t].reshape(width, cols))
            take('cg0')
        else:
            take(f'cg{t}')
            pushed = dot(schur_r[t].reshape(2 * 64, width), cost_g[t].reshape(width, cols))
            take(f'xg{t}')
        if t == T - 1:
            inj_add(t)
        if t == 0:
            pushed = dot(schur_r[t].reshape(2 * 64, width), cost_g[t].reshape(width, cols))
        else:
            moving = dot(gain_r[t].reshape(2 * 64, width), state_g[t].reshape(width, cols))
        full = moving - pushed
        full_v[t] = full.reshape(2, 64, cols)
        pend[f'full{t}'] = lambda t=t: landed(full_r.at[t], full_sem.at[t])
        far_copy(full_v.at[t, 1 - core], full_r.at[t], full_sem.at[t], x, 1 - core)
        if t == T - 1:
            inj_end(t)
        take(f'full{t}')
        total = full_v[t, core] + full_r[t]
        state_v[t] = total
        if t < T - 1:
            state_g[t + 1, spot] = total.astype(BF16)
            pend[f'xg{t + 1}'] = lambda t=t: plane_wait(state_g.at[t + 1], xg_sem.at[t + 1])
            plane_copy(lambda ss, t=t: state_g.at[t + 1, spot], state_g.at[t + 1, spot], xg_sem.at[t + 1])
            if t + 2 < T:
                send_cg(t + 2)
        pend[f'sout{t}'] = lambda t=t: home_wait(t, lambda: [landed(stor_out.at[0, :, lanes(xx)], sout_sem.at[xx]) for xx in range(X)])
        ring_copy(state_v.at[t], stor_out.at[0, :, lanes(x)], sout_sem.at[x], 2 * (t // 2) + core, t % 2)
        if t < T - 1:
            inj_add(t)
            inj_end(t)

    for t in range(T):
        take(f'inj{t}')
    network = weighted_v[...] - inj_r[...].astype(F32)
    network_v[...] = network.astype(BF16)
    store = pltpu.make_async_copy(network_v, network_out, load_sem.at[8])
    store.start()
    for t in range(T):
        take(f'cout{t}')
        take(f'sout{t}')
    store.wait()

    for key in list(pend):
        take(key)
    for on, copy, *more in sent:
        if more:
            if not more[0]:
                continue
            had = period == more[0][0]
            for p in more[0][1:]:
                had = had | (period == p)
            on = on & had
        if on is None:
            copy.wait_send()
        else:
            pl.when(on)(copy.wait_send)
    for send in plane_sent:
        plane_wait(rs_s.at[0], send)


def finish(stor, cost, network, inverse, stor_out, cost_out, upd_out, stor_v, cost_v, network_v, inv_v, upd_v, sem):
    pairs = ((network, network_v), (inverse, inv_v), (stor, stor_v), (cost, cost_v))
    loads = [pltpu.make_async_copy(src, dst, sem.at[i]) for i, (src, dst) in enumerate(pairs)]
    for load in loads:
        load.start()
    loads[0].wait()
    loads[1].wait()
    upd_v[0] = dot(inv_v[0], network_v[...])
    stores = [pltpu.make_async_copy(upd_v, upd_out, sem.at[4])]
    stores[0].start()
    for i, (src, dst) in enumerate(((stor_v, stor_out), (cost_v, cost_out))):
        loads[2 + i].wait()
        stores.append(pltpu.make_async_copy(src, dst, sem.at[5 + i]))
        stores[-1].start()
    for copy in stores:
        copy.wait()


def body(gain, schur, inverse_blocks, sensitivity, residual_bus, unit_rhs, start_state, active_set, unit_bus):
    anywhere = pl.BlockSpec(memory_space=pl.ANY)
    n = inverse_blocks.shape[1]
    dma = pltpu.SemaphoreType.DMA
    scratch = [
        pltpu.VMEM((2, n, 1024), BF16),
        pltpu.VMEM((2, 1024, n), BF16),
        pltpu.VMEM((n, 512), F32),
        pltpu.VMEM((n, n), BF16),
        pltpu.VMEM((1, n), jnp.int32),
        pltpu.VMEM((1, 2048), jnp.int32),
        pltpu.VMEM((64, 512), F32),
        pltpu.VMEM((64, 512), BF16),
        pltpu.VMEM((n, 512), F32),
        pltpu.VMEM((n, 512), BF16),
        pltpu.VMEM((2, n, 512), BF16),
        pltpu.VMEM((2, 64, 1024), BF16),
        pltpu.VMEM((2, 64, 1024), BF16),
        pltpu.VMEM((T, 2, 64, 1024), BF16),
        pltpu.VMEM((T, 2, 64, 1024), BF16),
        pltpu.VMEM((T - 1, 1024, 128), BF16),
        pltpu.VMEM((T, 64, 128), F32),
        pltpu.VMEM((1024, 384), F32),
        pltpu.VMEM((T, S, 64, 128), BF16),
        pltpu.VMEM((T, S, 64, 128), BF16),
        pltpu.VMEM((T, 64, 128), F32),
        pltpu.VMEM((T, S, 64, 128), BF16),
        pltpu.VMEM((T, 2, 64, 128), BF16),
        pltpu.VMEM((T, 64, 128), F32),
        pltpu.VMEM((T, S, 64, 128), BF16),
        pltpu.VMEM((T, 2, 64, 128), F32),
        pltpu.VMEM((T, 64, 128), F32),
        pltpu.VMEM((2 * n, 1024), BF16),
        pltpu.VMEM((T, 2, n, 128), BF16),
        pltpu.VMEM((T, n, 128), BF16),
        pltpu.VMEM((n, 512), BF16),
        pltpu.VMEM((n, 512), BF16),
        dma((9,)),
        dma((2,)),
        dma((8,)),
        dma((8,)),
        dma((8,)),
        dma((8,)),
        dma((4,)),
        dma((1,)),
        dma((4,)),
        dma((4,)),
        dma((4,)),
        dma((4,)),
        dma((4,)),
        dma((4,)),
        dma((4,)),
        dma((4,)),
        dma((4,)),
        dma((80,)),
        dma((12,)),
    ]
    moved = pl.pallas_call(
        kernel,
        out_shape=(
            jax.ShapeDtypeStruct((1, 64, 512), F32),
            jax.ShapeDtypeStruct((1, 64, 512), F32),
            jax.ShapeDtypeStruct((n, 512), BF16),
        ),
        in_specs=[anywhere] * 9,
        out_specs=(anywhere,) * 3,
        scratch_shapes=scratch,
        compiler_params=pltpu.CompilerParams(
            collective_id=0, has_side_effects=True, vmem_limit_bytes=60 * 1024 * 1024
        ),
    )(
        gain, schur, inverse_blocks, sensitivity, residual_bus, unit_rhs, start_state, active_set,
        unit_bus.reshape(1, -1),
    )
    return pl.pallas_call(
        finish,
        out_shape=(
            jax.ShapeDtypeStruct((1, 64, 512), F32),
            jax.ShapeDtypeStruct((1, 64, 512), F32),
            jax.ShapeDtypeStruct((1, n, 512), F32),
        ),
        in_specs=[anywhere] * 4,
        out_specs=(anywhere,) * 3,
        scratch_shapes=[
            pltpu.VMEM((1, 64, 512), F32),
            pltpu.VMEM((1, 64, 512), F32),
            pltpu.VMEM((n, 512), BF16),
            pltpu.VMEM((1, n, n), BF16),
            pltpu.VMEM((1, n, 512), F32),
            dma((7,)),
        ],
        compiler_params=pltpu.CompilerParams(vmem_limit_bytes=60 * 1024 * 1024),
    )(*moved, inverse_blocks)


def solution(mesh):
    placed = (
        P("period", "bus", None),
        P("period", "bus", None),
        P("period", "bus", None),
        P("bus", None),
        P("period", "bus", None),
        P("period", "bus", None),
        P("bus", None),
        P("period", "bus"),
        P(),
    )
    return jax.shard_map(
        body,
        mesh=mesh,
        in_specs=placed,
        out_specs=(P("period", "bus", None), P("period", "bus", None), P("period", "bus", None)),
        check_vma=False,
    )
```
